32 devices in a mesh: lat: 8 (over z, x), ch: 4 (over y, core).
Axes of the slice: x: 2, y: 2, z: 4, core: 2. Of those that a mesh axis runs over, the one named last changes fastest.
Arguments:
- tokens: bfloat16 [1, 16, 8, 69120], P(None, 'lat', 'ch'), may hold values from -6 to 6
- cotangent: bfloat16 [1, 16, 8, 69120], P(None, 'lat', 'ch'), may hold values from -6 to 6
- first_weight: bfloat16 [2, 8, 96, 96], P(None, 'ch'), may hold values from -0.4375 to 0.4375
- first_bias: bfloat16 [2, 8, 96], P(None, 'ch'), may hold values from -6 to 6
- second_weight: bfloat16 [2, 8, 96, 96], P(None, 'ch'), may hold values from -0.4375 to 0.4375
- relu_mask: int32 [1, 2, 8, 256, 1536], P(None, None, 'ch', 'lat'), may hold values 0 or 1
- shrink_mask: int32 [1, 2, 8, 256, 1536], P(None, None, 'ch', 'lat'), may hold values 0 or 1
Outputs:
- token_gradient: bfloat16 [1, 16, 8, 69120], P(None, 'lat', 'ch')
- first_gradient: float32 [2, 8, 96, 96], P(None, 'ch')
- bias_gradient: float32 [2, 8, 96], P(None, 'ch')
- second_gradient: float32 [2, 8, 96, 96], P(None, 'ch')
The draws below stay inside these ranges and needn't reach their ends.
All inputs are finite; a program needn't handle non-finite values. No bound on the sum of `relu_mask` or of `shrink_mask` on one device may be relied on, other than what follows from the above.
Results may differ from the reference program's by a relative error of at most 0.0093.
Values may be sent and summed in bfloat16 or wider, within the bound.
No kernel may reach another device: no remote copies, remote signals or barrier semaphores. Data moves between devices by JAX's collectives and lax.ppermute only.
A program may use at most 64 MiB of HBM per device.

```python
import math
import jax
import jax.numpy as jnp
from jax import lax

BLOCKS = 8
BLOCK_SIZE = 96
NLON = 720
WAVES = 256
SAMPLES = 1
NLAT = 16


def plant(values, stream_key, least, top_value):
    place = [jax.random.randint(jax.random.fold_in(stream_key, axis), (), 0, length) for axis, length in enumerate(values.shape)]
    main_axis = values.shape.index(max(values.shape))
    beside = place[:main_axis] + [(place[main_axis] + 1) % values.shape[main_axis]] + place[main_axis + 1:]
    return values.at[tuple(place)].set(least).at[tuple(beside)].set(top_value)


def block_scale(stream_key, shape, cuts, least, largest):
    level, own = 1.0, jax.random.fold_in(stream_key, 6)
    for axis_at, shards_of in cuts:
        draws = jnp.exp(jax.random.uniform(jax.random.fold_in(own, axis_at), (shards_of,), jnp.float32, least / len(cuts), largest / len(cuts)))
        level = level * jnp.repeat(draws, shape[axis_at] // shards_of).reshape([-1 if axis == axis_at else 1 for axis in range(len(shape))])
    return level


def centred(key, shape, spread, reach, shards=(), kind=jnp.bfloat16):
    loudness = block_scale(key, shape, shards, -0.22, 0.18) if shards else 1.0
    result = jax.random.normal(key, shape, jnp.float32) * spread * loudness
    return jnp.minimum(jnp.maximum(result, -reach), reach).astype(kind)


def setup_inputs(seed: int = 0) -> dict:
    arg_keys = jax.random.split(jax.random.key(seed), 8)
    return {
        "tokens": centred(arg_keys[0], (SAMPLES, NLAT, BLOCKS, NLON * BLOCK_SIZE), 1.0, 6.0, ((1, 8), (2, 4))),
        "cotangent": centred(arg_keys[1], (SAMPLES, NLAT, BLOCKS, NLON * BLOCK_SIZE), 1.0, 6.0, ((1, 8), (2, 4))),
        "first_weight": centred(arg_keys[2], (2, BLOCKS, BLOCK_SIZE, BLOCK_SIZE), (2 * BLOCK_SIZE) ** -0.5, 0.4375, ((1, 4),)),
        "first_bias": centred(arg_keys[3], (2, BLOCKS, BLOCK_SIZE), 1.0, 6.0, ((1, 4),)),
        "second_weight": centred(arg_keys[4], (2, BLOCKS, BLOCK_SIZE, BLOCK_SIZE), (2 * BLOCK_SIZE) ** -0.5, 0.4375, ((1, 4),)),
        "relu_mask": plant((jax.random.randint(arg_keys[5], (SAMPLES, 2, BLOCKS, WAVES, NLAT * BLOCK_SIZE), 0, 2) < 1).astype(jnp.int32), jax.random.fold_in(arg_keys[5], 1), 0, 1),
        "shrink_mask": plant((jax.random.randint(arg_keys[6], (SAMPLES, 2, BLOCKS, WAVES, NLAT * BLOCK_SIZE), 0, 4) < 3).astype(jnp.int32), jax.random.fold_in(arg_keys[6], 1), 0, 1),
    }


def east_basis(count, waves):
    column = jnp.arange(count, dtype=jnp.int32)[:, None]
    number = jnp.arange(waves, dtype=jnp.int32)[None, :]
    phase = (column * number % count).astype(jnp.float32) * (2.0 * math.pi / count)
    factor = 1.0 / math.sqrt(count)
    return jnp.stack([jnp.cos(phase) * factor, -jnp.sin(phase) * factor], axis=1)

def north_basis(count):
    column = jnp.arange(count, dtype=jnp.int32)[:, None]
    number = jnp.arange(count, dtype=jnp.int32)[None, :]
    phase = (column * number % count).astype(jnp.float32) * (2.0 * math.pi / count)
    factor = 1.0 / math.sqrt(count)
    cosine = jnp.cos(phase) * factor
    sine = jnp.sin(phase) * factor
    upper = jnp.concatenate([cosine, sine], axis=1)
    lower = jnp.concatenate([-sine, cosine], axis=1)
    return jnp.concatenate([upper, lower], axis=0)

def complex_mix(left_real, left_imag, right_real, right_imag, form):
    left_real = left_real.astype(jnp.float32)
    left_imag = left_imag.astype(jnp.float32)
    right_real = right_real.astype(jnp.float32)
    right_imag = right_imag.astype(jnp.float32)
    real_part = jnp.einsum(form, left_real, right_real) - jnp.einsum(form, left_imag, right_imag)
    imag_part = jnp.einsum(form, left_real, right_imag) + jnp.einsum(form, left_imag, right_real)
    return (real_part, imag_part)

def reference(tokens, cotangent, first_weight, first_bias, second_weight, relu_mask, shrink_mask):
    east_table = east_basis(NLON, WAVES).astype(jnp.bfloat16).astype(jnp.float32)
    north_table = north_basis(NLAT).astype(jnp.bfloat16).astype(jnp.float32)
    factor = 1.0 / math.sqrt(NLAT * WAVES)

    def by_block(field):
        return jnp.moveaxis(field.reshape(SAMPLES, NLAT, BLOCKS, NLON, BLOCK_SIZE), 2, 0)

    def mask_block(mask):
        grid = jnp.moveaxis(mask.reshape(SAMPLES, 2, BLOCKS, WAVES, NLAT, BLOCK_SIZE), 2, 0)
        grid = jnp.swapaxes(grid, 3, 4)
        return grid.reshape(BLOCKS, SAMPLES, 2, NLAT * WAVES, BLOCK_SIZE)

    def to_modes(field):
        spec = jnp.einsum('bhwe,wsk->bshke', field.astype(jnp.float32), east_table).astype(jnp.bfloat16)
        flat = spec.reshape(SAMPLES, 2 * NLAT, WAVES * BLOCK_SIZE).astype(jnp.float32)
        mixed = jnp.einsum('qp,bpn->bqn', north_table, flat).astype(jnp.bfloat16)
        return mixed.reshape(SAMPLES, 2, NLAT * WAVES, BLOCK_SIZE)

    def one_block(item):
        field, upper_grad, relu_part, shrink_part, weight_one, bias_one, weight_two = item
        relu_keep = relu_part.astype(jnp.float32)
        modes = to_modes(field)
        upstream = to_modes(upper_grad) * shrink_part.astype(jnp.bfloat16)
        before_real, before_imag = complex_mix(modes[:, 0], modes[:, 1], weight_one[0], weight_one[1], 'bme,ef->bmf')
        hidden_real = (relu_keep[:, 0] * (before_real + bias_one[0].astype(jnp.float32))).astype(jnp.bfloat16)
        hidden_imag = (relu_keep[:, 1] * (before_imag + bias_one[1].astype(jnp.float32))).astype(jnp.bfloat16)
        second_real, second_imag = complex_mix(hidden_real, -hidden_imag, upstream[:, 0], upstream[:, 1], 'bme,bmf->ef')
        second_grad = jnp.stack([second_real, second_imag]) * factor
        back_real, back_imag = complex_mix(upstream[:, 0], upstream[:, 1], weight_two[0], -weight_two[1], 'bmf,ef->bme')
        inner_real = (relu_keep[:, 0] * back_real).astype(jnp.bfloat16)
        inner_imag = (relu_keep[:, 1] * back_imag).astype(jnp.bfloat16)
        first_real, first_imag = complex_mix(modes[:, 0], -modes[:, 1], inner_real, inner_imag, 'bme,bmf->ef')
        first_grad = jnp.stack([first_real, first_imag]) * factor
        bias_grad = jnp.stack([lax.optimization_barrier(jnp.sum(inner_real.astype(jnp.float32), axis=(0, 1))), lax.optimization_barrier(jnp.sum(inner_imag.astype(jnp.float32), axis=(0, 1)))]) * factor
        mode_real, mode_imag = complex_mix(inner_real, inner_imag, weight_one[0], -weight_one[1], 'bmf,ef->bme')
        stacked = jnp.stack([mode_real, mode_imag], axis=1).astype(jnp.bfloat16)
        stacked = stacked.reshape(SAMPLES, 2 * NLAT, WAVES * BLOCK_SIZE).astype(jnp.float32)
        returned = jnp.einsum('qp,bqn->bpn', north_table, stacked).astype(jnp.bfloat16)
        returned = returned.reshape(SAMPLES, 2, NLAT, WAVES, BLOCK_SIZE).astype(jnp.float32)
        token_grad = jnp.einsum('bshke,wsk->bhwe', returned, east_table) + upper_grad.astype(jnp.float32)
        return (token_grad.astype(jnp.bfloat16), first_grad, bias_grad, second_grad)
    items = (by_block(tokens), by_block(cotangent), mask_block(relu_mask), mask_block(shrink_mask), jnp.moveaxis(first_weight, 1, 0), jnp.moveaxis(first_bias, 1, 0), jnp.moveaxis(second_weight, 1, 0))
    token_all, first_all, bias_all, second_all = lax.map(one_block, items)
    token_gradient = jnp.moveaxis(token_all, 0, 2).reshape(SAMPLES, NLAT, BLOCKS, NLON * BLOCK_SIZE)
    return (token_gradient, jnp.moveaxis(first_all, 0, 1), jnp.moveaxis(bias_all, 0, 1), jnp.moveaxis(second_all, 0, 1))
```

```python
import functools
import math

import jax
import jax.numpy as jnp
import numpy as np
from jax import lax
from jax.experimental import pallas as pl
from jax.experimental.pallas import tpu as pltpu
from jax.sharding import PartitionSpec as P

WAVES = 256
BF16 = jnp.bfloat16
F32 = jnp.float32


def group_of(wave_dev):
    return 16 if wave_dev % 16 == 0 else wave_dev


def east_rows(count, waves, owners):
    wave_dev = waves // owners
    group = group_of(wave_dev)
    phase = np.outer(np.arange(waves), np.arange(count)) % count * (2.0 * math.pi / count)
    table = np.stack([np.cos(phase), -np.sin(phase)]) / math.sqrt(count)
    table = table.reshape(2, owners, wave_dev // group, group, count)
    return table.transpose(1, 2, 0, 3, 4).reshape(2 * waves, count)


def north_rows(owners, rows, group):
    cells = owners * rows
    phase = np.outer(np.arange(cells), np.arange(cells)) % cells * (2.0 * math.pi / cells)
    cosine, sine = np.cos(phase) / math.sqrt(cells), np.sin(phase) / math.sqrt(cells)
    table = np.stack([np.stack([cosine, sine], 1), np.stack([-sine, cosine], 1)])
    table = table.reshape(2, cells, 2, owners, rows)
    full = np.einsum("tqsjr,kl->rtkqjsl", table, np.eye(group))
    return full.reshape(rows, 2 * group * cells, owners * 2 * group)


def dot(left, right, form=((1,), (0,))):
    return lax.dot_general(left, right, (form, ((), ())), preferred_element_type=F32)


ROWS, COLS = ((0,), (0,)), ((1,), (1,))


def mix_kernel(geo, spec_ref, table_ref, back_ref, weight_ref, bias_ref, relu_ref, shrink_ref,
               back_out, *rest):
    *grad_outs, first_sum, second_sum, bias_sum = rest
    owners, groups, group, rows, blocks, width, packed = geo
    span = owners * 2 * group
    half = table_ref.shape[1] // 2
    one_real, one_imag, two_real, two_imag = (weight_ref[i] for i in range(4))
    field = rows * width
    for g in range(groups):
        if groups == 1:
            spec = spec_ref[...]
        else:
            spec = spec_ref[...].reshape(owners, groups, 2 * group, 2 * field)
            spec = spec[:, g].reshape(span, 2 * field)

        def modes_of(base):
            total = None
            for r in range(rows):
                term = dot(table_ref[r], spec[:, base + r * width : base + (r + 1) * width])
                total = term if total is None else total + term
            return total.astype(BF16)

        at = slice(g * half, (g + 1) * half)
        modes = modes_of(0)
        spectral = modes_of(field)
        mode_real, mode_imag = modes[:half], modes[half:]
        relu_real = relu_ref[0, at, :].astype(F32)
        relu_imag = relu_ref[1, at, :].astype(F32)
        up_real = spectral[:half] * shrink_ref[0, at, :]
        up_imag = spectral[half:] * shrink_ref[1, at, :]
        hidden_real = dot(mode_real, one_real) - dot(mode_imag, one_imag) + bias_ref[0:1, :]
        hidden_imag = dot(mode_real, one_imag) + dot(mode_imag, one_real) + bias_ref[1:2, :]
        hidden_real = (relu_real * hidden_real).astype(BF16)
        hidden_imag = (relu_imag * hidden_imag).astype(BF16)
        inner_real = dot(up_real, two_real, COLS) + dot(up_imag, two_imag, COLS)
        inner_imag = dot(up_imag, two_real, COLS) - dot(up_real, two_imag, COLS)
        inner_real = (relu_real * inner_real).astype(BF16)
        inner_imag = (relu_imag * inner_imag).astype(BF16)
        grad_real = dot(inner_real, one_real, COLS) + dot(inner_imag, one_imag, COLS)
        grad_imag = dot(inner_imag, one_real, COLS) - dot(inner_real, one_imag, COLS)
        grad = jnp.concatenate([grad_real.astype(BF16), grad_imag.astype(BF16)], axis=0)
        back = [dot(back_ref[r], grad).astype(BF16) for r in range(rows)]
        back = jnp.concatenate(back, axis=1)
        if packed:
            back_out[:, g * 2 * group : (g + 1) * 2 * group, :] = back.reshape(
                owners, 2 * group, field
            )
        else:
            back_out[...] = back
        sums = (
            (second_sum, 0, dot(hidden_real, up_real, ROWS) + dot(hidden_imag, up_imag, ROWS)),
            (second_sum, 1, dot(hidden_real, up_imag, ROWS) - dot(hidden_imag, up_real, ROWS)),
            (first_sum, 0, dot(mode_real, inner_real, ROWS) + dot(mode_imag, inner_imag, ROWS)),
            (first_sum, 1, dot(mode_real, inner_imag, ROWS) - dot(mode_imag, inner_real, ROWS)),
            (bias_sum, 0, jnp.sum(inner_real.astype(F32), axis=0, keepdims=True)),
            (bias_sum, 1, jnp.sum(inner_imag.astype(F32), axis=0, keepdims=True)),
        )
        for ref, part, value in sums:
            ref[part] = value if g == 0 else ref[part] + value
    block = width // blocks
    lanes = lax.broadcasted_iota(jnp.int32, (block, width), 1)

    def diagonal(ref, part):
        value = ref[part, :block, :]
        for n in range(1, blocks):
            value = jnp.where(lanes < n * block, value, ref[part, n * block : (n + 1) * block, :])
        return value

    gathered = jnp.concatenate(
        [
            jnp.concatenate([diagonal(ref, 0), diagonal(ref, 1)], axis=1)
            for ref in (first_sum, second_sum)
        ],
        axis=0,
    ).astype(BF16)
    bias = jnp.concatenate([bias_sum[0], bias_sum[1]], axis=1).astype(BF16)
    if packed:
        per = 2 * block // owners
        start = groups * 2 * group
        tail = back_out.shape[1] - start - per
        bias = jnp.broadcast_to(bias, (tail, field))
        for j in range(owners):
            chunk = jnp.concatenate([gathered[j * per : (j + 1) * per], bias], axis=0)
            back_out[j, start:, :] = chunk
    else:
        grad_outs[0][...] = gathered
        grad_outs[1][...] = bias


def local(tokens, cotangent, first_weight, first_bias, second_weight, relu_mask, shrink_mask):
    batches, rows, blocks, flat_east = tokens.shape
    block = first_weight.shape[2]
    cells = flat_east // block
    owners = lax.axis_size("lat")
    wave_dev = WAVES // owners
    group = group_of(wave_dev)
    groups = wave_dev // group
    north = rows * owners
    width = blocks * block
    field = rows * width
    factor = 1.0 / math.sqrt(north * WAVES)

    east = jnp.asarray(east_rows(cells, WAVES, owners), BF16)
    table = north_rows(owners, rows, group)
    forward = jnp.asarray(table, BF16)
    backward = jnp.asarray(table.transpose(0, 2, 1), BF16)

    grid = jnp.stack([tokens, cotangent]).reshape(2, rows, blocks, cells, block)
    grid = grid.transpose(3, 0, 1, 2, 4).reshape(cells, 2 * field)
    waves = jnp.dot(east, grid, preferred_element_type=F32).astype(BF16)
    span = 2 * wave_dev
    waves = waves.reshape(owners, span, 2 * field)
    waves = lax.all_to_all(waves, "lat", split_axis=0, concat_axis=0, tiled=True)

    def by_mode(mask):
        mask = mask.astype(BF16).reshape(2, blocks, wave_dev, north, block)
        return mask.transpose(0, 2, 3, 1, 4).reshape(2, wave_dev * north, width)

    def diagonal(weight):
        eye = jnp.eye(blocks, dtype=weight.dtype)
        spread = weight[:, :, :, None, :] * eye[None, :, None, :, None]
        return spread.reshape(2, width, width)

    weights = jnp.concatenate([diagonal(first_weight), diagonal(second_weight)])
    bias = first_bias.reshape(2, width).astype(F32)

    packed = (2 * group) % 16 == 0 and (2 * block) % owners == 0
    per = -(-2 * block // owners)
    extra = -(-(per + 1) // 16) * 16 - per if packed else 1
    shapes = ((owners, span + per + extra, field),) if packed else (
        (owners * span, field), (2 * block, field), (1, field))
    vmem = pl.BlockSpec(memory_space=pltpu.VMEM)
    sent, *parts = pl.pallas_call(
        functools.partial(mix_kernel, (owners, groups, group, rows, blocks, width, packed)),
        out_shape=[jax.ShapeDtypeStruct(shape, BF16) for shape in shapes],
        in_specs=[vmem] * 7,
        out_specs=[vmem] * len(shapes),
        scratch_shapes=[
            pltpu.VMEM((2, width, width), F32),
            pltpu.VMEM((2, width, width), F32),
            pltpu.VMEM((2, 1, width), F32),
        ],
        name="mix",
    )(waves.reshape(owners * span, 2 * field), forward, backward, weights, bias,
      by_mode(relu_mask), by_mode(shrink_mask))
    if not packed:
        grads = jnp.pad(parts[0], ((0, owners * per - 2 * block), (0, 0)))
        biases = jnp.broadcast_to(parts[1][None], (owners, 1, field))
        sent = sent.reshape(owners, span, field)
        sent = jnp.concatenate([sent, grads.reshape(owners, per, field), biases], axis=1)
    returned = lax.all_to_all(sent, "lat", split_axis=0, concat_axis=0, tiled=True)
    back = returned[:, :span].reshape(owners * span, field)
    chunk = jnp.sum(returned[:, span:].astype(F32), axis=0) * factor
    chunk = jnp.broadcast_to(chunk.astype(BF16)[None], (owners,) + chunk.shape)
    totals = lax.all_to_all(chunk, "lat", split_axis=0, concat_axis=0, tiled=True).astype(F32)

    token = lax.dot_general(east, back, (((0,), (0,)), ((), ())), preferred_element_type=F32)
    token = (token + grid[:, field:].astype(F32)).astype(BF16)
    token = token.reshape(cells, rows, blocks, block).transpose(1, 2, 0, 3)
    token = token.reshape(batches, rows, blocks, flat_east)

    grads = totals[:, :per].reshape(owners * per, field)[: 2 * block]
    grads = grads.reshape(2, block, 2, blocks, block).transpose(0, 2, 3, 1, 4)
    bias_grad = totals[0, per].reshape(2, blocks, block)
    return (token, grads[0], bias_grad, grads[1])


def solution(mesh):
    return jax.shard_map(
        local,
        mesh=mesh,
        in_specs=(
            P(None, "lat", "ch", None),
            P(None, "lat", "ch", None),
            P(None, "ch", None, None),
            P(None, "ch", None),
            P(None, "ch", None, None),
            P(None, None, "ch", "lat", None),
            P(None, None, "ch", "lat", None),
        ),
        out_specs=(
            P(None, "lat", "ch", None),
            P(None, "ch", None, None),
            P(None, "ch", None),
            P(None, "ch", None, None),
        ),
        check_vma=False,
    )
```

```python
import functools
import math

import jax
import jax.numpy as jnp
import numpy as np
from jax import lax
from jax.experimental import pallas as pl
from jax.experimental.pallas import tpu as pltpu
from jax.sharding import PartitionSpec as P

WAVES = 256
BF16 = jnp.bfloat16
F32 = jnp.float32


def group_of(wave_dev):
    return 16 if wave_dev % 16 == 0 else wave_dev


def east_rows(count, waves, owners):
    wave_dev = waves // owners
    group = group_of(wave_dev)
    phase = np.outer(np.arange(waves), np.arange(count)) % count * (2.0 * math.pi / count)
    table = np.stack([np.cos(phase), -np.sin(phase)]) / math.sqrt(count)
    table = table.reshape(2, owners, wave_dev // group, group, count)
    return table.transpose(1, 2, 0, 3, 4).reshape(2 * waves, count)


def north_rows(owners, rows, group):
    cells = owners * rows
    phase = np.outer(np.arange(cells), np.arange(cells)) % cells * (2.0 * math.pi / cells)
    cosine, sine = np.cos(phase) / math.sqrt(cells), np.sin(phase) / math.sqrt(cells)
    table = np.stack([np.stack([cosine, sine], 1), np.stack([-sine, cosine], 1)])
    table = table.reshape(2, cells, 2, owners, rows)
    full = np.einsum("tqsjr,kl->rtqkjsl", table, np.eye(group))
    return full.reshape(rows, 2 * group * cells, owners * 2 * group)


def dot(left, right, form=((1,), (0,))):
    return lax.dot_general(left, right, (form, ((), ())), preferred_element_type=F32)


ROWS, COLS = ((0,), (0,)), ((1,), (1,))


def mix_group(geo, spec, refs, g):
    rows, width = geo
    table_ref, back_ref, weight_ref, bias_ref, relu_ref, shrink_ref = refs
    half = table_ref.shape[1] // 2
    one_real, one_imag, two_real, two_imag = (weight_ref[i] for i in range(4))
    field = rows * width

    def modes_of(base):
        total = None
        for r in range(rows):
            term = dot(table_ref[r], spec[:, base + r * width : base + (r + 1) * width])
            total = term if total is None else total + term
        return total.astype(BF16)

    at = slice(g * half, (g + 1) * half)
    modes = modes_of(0)
    spectral = modes_of(field)
    mode_real, mode_imag = modes[:half], modes[half:]
    relu_real = relu_ref[0, at, :].astype(F32)
    relu_imag = relu_ref[1, at, :].astype(F32)
    up_real = spectral[:half] * shrink_ref[0, at, :]
    up_imag = spectral[half:] * shrink_ref[1, at, :]
    hidden_real = dot(mode_real, one_real) - dot(mode_imag, one_imag) + bias_ref[0:1, :].astype(F32)
    hidden_imag = dot(mode_real, one_imag) + dot(mode_imag, one_real) + bias_ref[1:2, :].astype(F32)
    hidden_real = (relu_real * hidden_real).astype(BF16)
    hidden_imag = (relu_imag * hidden_imag).astype(BF16)
    inner_real = dot(up_real, two_real, COLS) + dot(up_imag, two_imag, COLS)
    inner_imag = dot(up_imag, two_real, COLS) - dot(up_real, two_imag, COLS)
    inner_real = (relu_real * inner_real).astype(BF16)
    inner_imag = (relu_imag * inner_imag).astype(BF16)
    grad_real = dot(inner_real, one_real, COLS) + dot(inner_imag, one_imag, COLS)
    grad_imag = dot(inner_imag, one_real, COLS) - dot(inner_real, one_imag, COLS)
    grad = jnp.concatenate([grad_real.astype(BF16), grad_imag.astype(BF16)], axis=0)
    back = [dot(back_ref[r], grad).astype(BF16) for r in range(rows)]
    back = jnp.concatenate(back, axis=1)
    sums = (
        dot(mode_real, inner_real, ROWS) + dot(mode_imag, inner_imag, ROWS),
        dot(mode_real, inner_imag, ROWS) - dot(mode_imag, inner_real, ROWS),
        dot(hidden_real, up_real, ROWS) + dot(hidden_imag, up_imag, ROWS),
        dot(hidden_real, up_imag, ROWS) - dot(hidden_imag, up_real, ROWS),
        jnp.sum(inner_real.astype(F32), axis=0, keepdims=True),
        jnp.sum(inner_imag.astype(F32), axis=0, keepdims=True),
    )
    return back, sums


def gather_sums(sums, blocks):
    width = sums[0].shape[0]
    block = width // blocks
    lanes = lax.broadcasted_iota(jnp.int32, (block, width), 1)

    def diagonal(product):
        value = product[:block, :]
        for n in range(1, blocks):
            value = jnp.where(lanes < n * block, value, product[n * block : (n + 1) * block, :])
        return value

    gathered = [jnp.concatenate([diagonal(sums[i]), diagonal(sums[i + 1])], 1) for i in (0, 2)]
    return jnp.concatenate(gathered, axis=0), jnp.concatenate(sums[4:], axis=1)


def mix_whole_kernel(geo, spec_ref, *refs):
    rows, blocks, width = geo
    back, sums = mix_group((rows, width), spec_ref[...], refs[:6], 0)
    refs[6][...] = back
    gathered, bias = gather_sums(sums, blocks)
    refs[7][...] = gathered.astype(BF16)
    refs[8][...] = bias.astype(BF16)


def ready_kernel(geo, relu_in, shrink_in, first_in, second_in, bias_in,
                 relu_out, shrink_out, weight_out, bias_out):
    groups, group, north, blocks, block = geo
    for source, out in ((relu_in, relu_out), (shrink_in, shrink_out)):
        for s in range(2):
            planes = [source[0, s, n].astype(F32).astype(BF16) for n in range(blocks)]
            for q in range(north):
                at = slice(q * block, (q + 1) * block)
                row = jnp.concatenate([plane[:, at] for plane in planes], axis=1)
                for g in range(groups):
                    start = (g * north + q) * group
                    out[s, start : start + group, :] = row[g * group : (g + 1) * group]
    for index, source in enumerate((first_in, second_in)):
        for s in range(2):
            for n in range(blocks):
                parts = [source[s, n] if m == n else jnp.zeros((block, block), BF16)
                         for m in range(blocks)]
                at = slice(n * block, (n + 1) * block)
                weight_out[2 * index + s, at, :] = jnp.concatenate(parts, axis=1)
    for s in range(2):
        parts = [bias_in[s, n : n + 1, :] for n in range(blocks)]
        bias_out[s : s + 1, :] = jnp.concatenate(parts, axis=1)


def send_kernel(owners, grid_ref, east_ref, *refs):
    outs, scratch = refs[:-1], refs[-1]
    me = lax.axis_index("lat")
    scratch[...] = dot(east_ref[...], grid_ref[...]).astype(BF16)
    span = scratch.shape[0] // owners
    for d in range(owners):
        start = pl.multiple_of((me ^ d) * span, span)
        outs[d][...] = scratch[pl.ds(start, span), :]


def mix_kernel(geo, *refs):
    owners, groups, rows, blocks, width, per = geo
    pieces, consts, outs = refs[:owners], refs[owners : owners + 6], refs[owners + 6 : -3]
    spec_ref, back_ref, grad_ref = refs[-3:]
    me = lax.axis_index("lat")
    part = pieces[0].shape[0] // groups
    for d in range(owners):
        start = pl.multiple_of((me ^ d) * part, part)
        for g in range(groups):
            spec_ref[g, pl.ds(start, part), :] = pieces[d][g * part : (g + 1) * part, :]
    total = None
    for g in range(groups):
        back, sums = mix_group((rows, width), spec_ref[g], consts, g)
        back_ref[g] = back
        total = sums if total is None else [a + b for a, b in zip(total, sums)]
    grad_ref[...], bias = gather_sums(total, blocks)
    span = part * groups
    for d in range(owners):
        start = pl.multiple_of((me ^ d) * part, part)
        for g in range(groups):
            outs[d][g * part : (g + 1) * part, :] = back_ref[g, pl.ds(start, part), :]
        start = pl.multiple_of((me ^ d) * per, per)
        extra = jnp.broadcast_to(bias, (outs[d].shape[0] - span - per, bias.shape[1]))
        chunk = jnp.concatenate([grad_ref[pl.ds(start, per), :], extra], axis=0)
        outs[d][span:, :] = chunk.astype(BF16)


def sum_kernel(span, factor, *refs):
    pieces, out = refs[:-1], refs[-1]
    total = pieces[0][span:, :].astype(F32)
    for piece in pieces[1:]:
        total = total + piece[span:, :].astype(F32)
    total = (total * factor).astype(BF16)
    for d in range(out.shape[0]):
        out[d] = total


def token_kernel(owners, east_ref, grid_ref, *refs):
    pieces, out, scratch = refs[:owners], refs[owners], refs[owners + 1]
    me = lax.axis_index("lat")
    span = scratch.shape[0] // owners
    for d in range(owners):
        start = pl.multiple_of((me ^ d) * span, span)
        scratch[pl.ds(start, span), :] = pieces[d][:span, :]
    field = scratch.shape[1]
    token = dot(east_ref[...], scratch[...])
    out[...] = (token + grid_ref[:, field:].astype(F32)).astype(BF16)


VMEM = pl.BlockSpec(memory_space=pltpu.VMEM)


def call(kernel, args, shapes, scratch=(), name=None):
    return pl.pallas_call(
        kernel,
        out_shape=[jax.ShapeDtypeStruct(shape, BF16) for shape in shapes],
        in_specs=[VMEM] * len(args),
        out_specs=[VMEM] * len(shapes),
        scratch_shapes=[pltpu.VMEM(shape, kind) for shape, kind in scratch],
        name=name,
        compiler_params=pltpu.CompilerParams(vmem_limit_bytes=24 << 20),
    )(*args)


def swap(pieces, owners):
    return [pieces[0]] + [
        lax.ppermute(pieces[d], "lat", [(i, i ^ d) for i in range(owners)])
        for d in range(1, owners)
    ]


def local(tokens, cotangent, first_weight, first_bias, second_weight, relu_mask, shrink_mask):
    batches, rows, blocks, flat_east = tokens.shape
    block = first_weight.shape[2]
    cells = flat_east // block
    owners = lax.axis_size("lat")
    wave_dev = WAVES // owners
    group = group_of(wave_dev)
    groups = wave_dev // group
    north = rows * owners
    width = blocks * block
    field = rows * width
    span = 2 * wave_dev
    factor = 1.0 / math.sqrt(north * WAVES)

    east = east_rows(cells, WAVES, owners)
    east_back = jnp.asarray(east.T, BF16)
    east = jnp.asarray(east, BF16)
    table = north_rows(owners, rows, group)
    forward = jnp.asarray(table, BF16)
    backward = jnp.asarray(table.transpose(0, 2, 1), BF16)

    grid = jnp.stack([tokens, cotangent]).reshape(2, rows, blocks, cells, block)
    grid = grid.transpose(3, 0, 1, 2, 4).reshape(cells, 2 * field)

    def by_mode(mask):
        mask = mask.astype(BF16).reshape(2, blocks, groups, group, north, block)
        return mask.transpose(0, 2, 4, 3, 1, 5).reshape(2, wave_dev * north, width)

    def diagonal(weight):
        eye = jnp.eye(blocks, dtype=weight.dtype)
        spread = weight[:, :, :, None, :] * eye[None, :, None, :, None]
        return spread.reshape(2, width, width)

    per = -(-2 * block // owners)
    pairwise = owners in (2, 4, 8) and (2 * group) % 16 == 0 and per * owners == 2 * block

    if pairwise:
        extra = -(-(per + 1) // 16) * 16 - per
        modes = (2, wave_dev * north, width)
        relu, shrink, weights, bias = call(
            functools.partial(ready_kernel, (groups, group, north, blocks, block)),
            [relu_mask, shrink_mask, first_weight, second_weight, first_bias],
            [modes, modes, (4, width, width), (2, width)], name="ready",
        )
        consts = [forward, backward, weights, bias, relu, shrink]
        pieces = call(
            functools.partial(send_kernel, owners), [grid, east],
            [(span, 2 * field)] * owners, [((owners * span, 2 * field), BF16)], "send",
        )
        part = 2 * group
        pieces = call(
            functools.partial(mix_kernel, (owners, groups, rows, blocks, width, per)),
            swap(pieces, owners) + consts, [(span + per + extra, field)] * owners,
            [((groups, owners * part, 2 * field), BF16), ((groups, owners * part, field), BF16),
             ((2 * block, field), F32)], "mix",
        )
        pieces = swap(pieces, owners)
        (chunk,) = call(
            functools.partial(sum_kernel, span, factor), pieces,
            [(owners, per + extra, field)], name="total",
        )
        totals = lax.all_to_all(chunk, "lat", split_axis=0, concat_axis=0, tiled=True)
        (token,) = call(
            functools.partial(token_kernel, owners), [east_back, grid] + pieces,
            [(cells, field)], [((owners * span, field), BF16)], "token",
        )
    else:
        weights = jnp.concatenate([diagonal(first_weight), diagonal(second_weight)])
        bias = first_bias.reshape(2, width)
        consts = [forward, backward, weights, bias, by_mode(relu_mask), by_mode(shrink_mask)]
        waves = jnp.dot(east, grid, preferred_element_type=F32).astype(BF16)
        waves = waves.reshape(owners, span, 2 * field)
        waves = lax.all_to_all(waves, "lat", split_axis=0, concat_axis=0, tiled=True)
        waves = waves.reshape(owners, groups, 2 * group, 2 * field).swapaxes(0, 1)
        sent, grads, biases = [], 0.0, 0.0
        half = group * north
        for g in range(groups):
            at = slice(g * half, (g + 1) * half)
            some = consts[:4] + [mask[:, at] for mask in consts[4:]]
            back, grad, row = call(
                functools.partial(mix_whole_kernel, (rows, blocks, width)),
                [waves[g].reshape(owners * 2 * group, 2 * field)] + some,
                [(owners * 2 * group, field), (2 * block, field), (1, field)], name="mix",
            )
            sent.append(back.reshape(owners, 2 * group, field))
            grads, biases = grads + grad.astype(F32), biases + row.astype(F32)
        grads = jnp.pad(grads, ((0, owners * per - 2 * block), (0, 0)))
        biases = jnp.broadcast_to(biases[None], (owners, 1, field))
        sums = jnp.concatenate([grads.reshape(owners, per, field), biases], axis=1)
        sent = jnp.concatenate(sent + [sums.astype(BF16)], axis=1)
        returned = lax.all_to_all(sent, "lat", split_axis=0, concat_axis=0, tiled=True)
        back = returned[:, :span].reshape(owners * span, field)
        chunk = jnp.sum(returned[:, span:].astype(F32), axis=0) * factor
        chunk = jnp.broadcast_to(chunk.astype(BF16)[None], (owners,) + chunk.shape)
        totals = lax.all_to_all(chunk, "lat", split_axis=0, concat_axis=0, tiled=True)
        token = jnp.dot(east_back, back, preferred_element_type=F32)
        token = (token + grid[:, field:].astype(F32)).astype(BF16)

    token = token.reshape(cells, rows, blocks, block).transpose(1, 2, 0, 3)
    token = token.reshape(batches, rows, blocks, flat_east)
    totals = totals.astype(F32)
    grads = totals[:, :per].reshape(owners * per, field)[: 2 * block]
    grads = grads.reshape(2, block, 2, blocks, block).transpose(0, 2, 3, 1, 4)
    bias_grad = totals[0, per].reshape(2, blocks, block)
    return (token, grads[0], bias_grad, grads[1])


def solution(mesh):
    return jax.shard_map(
        local,
        mesh=mesh,
        in_specs=(
            P(None, "lat", "ch", None),
            P(None, "lat", "ch", None),
            P(None, "ch", None, None),
            P(None, "ch", None),
            P(None, "ch", None, None),
            P(None, None, "ch", "lat", None),
            P(None, None, "ch", "lat", None),
        ),
        out_specs=(
            P(None, "lat", "ch", None),
            P(None, "ch", None, None),
            P(None, "ch", None),
            P(None, "ch", None, None),
        ),
        check_vma=False,
    )
```

```python
import functools
import math

import jax
import jax.numpy as jnp
import numpy as np
from jax import lax
from jax.experimental import pallas as pl
from jax.experimental.pallas import tpu as pltpu
from jax.sharding import PartitionSpec as P

WAVES = 256
GO_ORDER = (0, 4, 6, 5, 7, 2, 3, 1)
BACK_ORDER = (0, 6, 7, 4, 5, 2, 3, 1)
BF16 = jnp.bfloat16
F32 = jnp.float32


def group_of(wave_dev):
    return 16 if wave_dev % 16 == 0 else wave_dev


def east_rows(count, waves, owners):
    wave_dev = waves // owners
    group = group_of(wave_dev)
    phase = np.outer(np.arange(waves), np.arange(count)) % count * (2.0 * math.pi / count)
    table = np.stack([np.cos(phase), -np.sin(phase)]) / math.sqrt(count)
    table = table.reshape(2, owners, wave_dev // group, group, count)
    return table.transpose(1, 2, 0, 3, 4).reshape(2 * waves, count)


def north_rows(owners, rows, group):
    cells = owners * rows
    phase = np.outer(np.arange(cells), np.arange(cells)) % cells * (2.0 * math.pi / cells)
    cosine, sine = np.cos(phase) / math.sqrt(cells), np.sin(phase) / math.sqrt(cells)
    table = np.stack([np.stack([cosine, sine], 1), np.stack([-sine, cosine], 1)])
    table = table.reshape(2, cells, 2, owners, rows)
    full = np.einsum("tqsjr,kl->rtqkjsl", table, np.eye(group))
    return full.reshape(rows, 2 * group * cells, owners * 2 * group)


def distances(order, owners):
    return [d for d in order if d < owners]


def dot(left, right, form=((1,), (0,))):
    return lax.dot_general(left, right, (form, ((), ())), preferred_element_type=F32)


ROWS, COLS = ((0,), (0,)), ((1,), (1,))


def mix_group(geo, spec, refs, g):
    rows, width = geo
    table_ref, back_ref, weight_ref, bias_ref, relu_ref, shrink_ref = refs
    half = table_ref.shape[1] // 2
    one_real, one_imag, two_real, two_imag = (weight_ref[i] for i in range(4))
    field = rows * width

    def modes_of(base):
        total = None
        for r in range(rows):
            term = dot(table_ref[r], spec[:, base + r * width : base + (r + 1) * width])
            total = term if total is None else total + term
        return total.astype(BF16)

    at = slice(g * half, (g + 1) * half)
    modes = modes_of(0)
    spectral = modes_of(field)
    mode_real, mode_imag = modes[:half], modes[half:]
    relu_real = relu_ref[0, at, :].astype(F32)
    relu_imag = relu_ref[1, at, :].astype(F32)
    up_real = spectral[:half] * shrink_ref[0, at, :]
    up_imag = spectral[half:] * shrink_ref[1, at, :]
    hidden_real = dot(mode_real, one_real) - dot(mode_imag, one_imag) + bias_ref[0:1, :].astype(F32)
    hidden_imag = dot(mode_real, one_imag) + dot(mode_imag, one_real) + bias_ref[1:2, :].astype(F32)
    hidden_real = (relu_real * hidden_real).astype(BF16)
    hidden_imag = (relu_imag * hidden_imag).astype(BF16)
    inner_real = dot(up_real, two_real, COLS) + dot(up_imag, two_imag, COLS)
    inner_imag = dot(up_imag, two_real, COLS) - dot(up_real, two_imag, COLS)
    inner_real = (relu_real * inner_real).astype(BF16)
    inner_imag = (relu_imag * inner_imag).astype(BF16)
    grad_real = dot(inner_real, one_real, COLS) + dot(inner_imag, one_imag, COLS)
    grad_imag = dot(inner_imag, one_real, COLS) - dot(inner_real, one_imag, COLS)
    grad = jnp.concatenate([grad_real.astype(BF16), grad_imag.astype(BF16)], axis=0)
    back = [dot(back_ref[r], grad).astype(BF16) for r in range(rows)]
    back = jnp.concatenate(back, axis=1)
    sums = (
        dot(mode_real, inner_real, ROWS) + dot(mode_imag, inner_imag, ROWS),
        dot(mode_real, inner_imag, ROWS) - dot(mode_imag, inner_real, ROWS),
        dot(hidden_real, up_real, ROWS) + dot(hidden_imag, up_imag, ROWS),
        dot(hidden_real, up_imag, ROWS) - dot(hidden_imag, up_real, ROWS),
        jnp.sum(inner_real.astype(F32), axis=0, keepdims=True),
        jnp.sum(inner_imag.astype(F32), axis=0, keepdims=True),
    )
    return back, sums


def gather_sums(sums, blocks):
    width = sums[0].shape[0]
    block = width // blocks
    lanes = lax.broadcasted_iota(jnp.int32, (block, width), 1)

    def diagonal(product):
        value = product[:block, :]
        for n in range(1, blocks):
            value = jnp.where(lanes < n * block, value, product[n * block : (n + 1) * block, :])
        return value

    gathered = [jnp.concatenate([diagonal(sums[i]), diagonal(sums[i + 1])], 1) for i in (0, 2)]
    return jnp.concatenate(gathered, axis=0), jnp.concatenate(sums[4:], axis=1)


def mix_whole_kernel(geo, spec_ref, *refs):
    rows, blocks, width = geo
    back, sums = mix_group((rows, width), spec_ref[...], refs[:6], 0)
    refs[6][...] = back
    gathered, bias = gather_sums(sums, blocks)
    refs[7][...] = gathered.astype(BF16)
    refs[8][...] = bias.astype(BF16)


def ready_kernel(geo, relu_in, shrink_in, first_in, second_in, bias_in,
                 relu_out, shrink_out, weight_out, bias_out):
    groups, group, north, blocks, block = geo
    for source, out in ((relu_in, relu_out), (shrink_in, shrink_out)):
        for s in range(2):
            planes = [source[0, s, n].astype(F32).astype(BF16) for n in range(blocks)]
            for q in range(north):
                at = slice(q * block, (q + 1) * block)
                row = jnp.concatenate([plane[:, at] for plane in planes], axis=1)
                for g in range(groups):
                    start = (g * north + q) * group
                    out[s, start : start + group, :] = row[g * group : (g + 1) * group]
    for index, source in enumerate((first_in, second_in)):
        for s in range(2):
            for n in range(blocks):
                parts = [source[s, n] if m == n else jnp.zeros((block, block), BF16)
                         for m in range(blocks)]
                at = slice(n * block, (n + 1) * block)
                weight_out[2 * index + s, at, :] = jnp.concatenate(parts, axis=1)
    for s in range(2):
        parts = [bias_in[s, n : n + 1, :] for n in range(blocks)]
        bias_out[s : s + 1, :] = jnp.concatenate(parts, axis=1)


def send_kernel(geo, tokens_ref, cotangent_ref, east_ref, *refs):
    owners, block, units, padded, tiles, unit = geo
    outs, kept_ref = refs[:-7], refs[-7]
    flat_ref, grid_ref, wave_ref, fields_ref, table_ref, sems = refs[-6:]
    rows, blocks = tokens_ref.shape[:2]
    field = rows * blocks * block
    copies = [
        pltpu.make_async_copy(tokens_ref, fields_ref.at[0], sems.at[0]),
        pltpu.make_async_copy(cotangent_ref, fields_ref.at[1], sems.at[1]),
        pltpu.make_async_copy(east_ref, table_ref, sems.at[2]),
    ]
    for copy in copies:
        copy.start()
    for f in range(2):
        copies[f].wait()
        source = fields_ref.at[f]
        places = []
        for h in range(rows):
            flat = source[h].astype(F32)
            flat_ref[f, h] = flat.reshape(blocks, units * tiles, 128)
            for n in range(blocks):
                parts = [flat_ref[f, h, n, pl.ds(c, units, stride=tiles), :].astype(BF16)
                         for c in range(tiles)]
                places.append(jnp.concatenate(parts, axis=1))
        for r in range(unit):
            piece = [place[:, r * block : (r + 1) * block] for place in places]
            at = slice(f * field, (f + 1) * field)
            grid_ref[r * padded : r * padded + units, at] = jnp.concatenate(piece, axis=1)
            if padded > units:
                grid_ref[r * padded + units : (r + 1) * padded, at] = jnp.zeros(
                    (padded - units, field), BF16)
    kept_ref[...] = grid_ref[:, field:]
    copies[2].wait()
    waves = dot(table_ref[...], grid_ref[...]).astype(BF16)
    if len(outs) == 1:
        outs[0][...] = waves
        return
    wave_ref[...] = waves
    me = lax.axis_index("lat")
    span = wave_ref.shape[0] // owners
    for d, distance in enumerate(distances(GO_ORDER, owners)):
        start = pl.multiple_of((me ^ distance) * span, span)
        outs[d][...] = wave_ref[pl.ds(start, span), :]


def mix_kernel(geo, *refs):
    owners, groups, rows, blocks, width, per = geo
    pieces, consts, outs = refs[:owners], refs[owners : owners + 6], refs[owners + 6 : -3]
    spec_ref, back_ref, grad_ref = refs[-3:]
    me = lax.axis_index("lat")
    part = pieces[0].shape[0] // groups
    for d, distance in enumerate(distances(GO_ORDER, owners)):
        start = pl.multiple_of((me ^ distance) * part, part)
        for g in range(groups):
            spec_ref[g, pl.ds(start, part), :] = pieces[d][g * part : (g + 1) * part, :]
    total = None
    for g in range(groups):
        back, sums = mix_group((rows, width), spec_ref[g], consts, g)
        back_ref[g] = back
        total = sums if total is None else [a + b for a, b in zip(total, sums)]
    grad_ref[...], bias = gather_sums(total, blocks)
    span = part * groups
    for d, distance in enumerate(distances(BACK_ORDER, owners)):
        start = pl.multiple_of((me ^ distance) * part, part)
        for g in range(groups):
            outs[d][g * part : (g + 1) * part, :] = back_ref[g, pl.ds(start, part), :]
        start = pl.multiple_of((me ^ distance) * per, per)
        extra = jnp.broadcast_to(bias, (outs[d].shape[0] - span - per, bias.shape[1]))
        chunk = jnp.concatenate([grad_ref[pl.ds(start, per), :], extra], axis=0)
        outs[d][span:, :] = chunk.astype(BF16)


def sum_kernel(geo, *refs):
    span, per, block, factor = geo
    pieces, out, bias_ref = refs[:-2], refs[-2], refs[-1]
    total = pieces[0][span:, :].astype(F32)
    for piece in pieces[1:]:
        total = total + piece[span:, :].astype(F32)
    total = total * factor
    chunk = total[:per].astype(BF16)
    for d in range(out.shape[0]):
        out[d] = chunk
    blocks = bias_ref.shape[1]
    lead = total[per : per + 1, :]
    for p in range(2):
        for n in range(blocks):
            at = slice((p * blocks + n) * block, (p * blocks + n + 1) * block)
            bias_ref[p, n : n + 1, :] = lead[:, at]


def token_kernel(geo, east_ref, kept_ref, *refs):
    owners, block, units, padded, tiles, unit = geo
    pieces, out, (wave_ref, flat_ref) = refs[:-3], refs[-3], refs[-2:]
    if len(pieces) == 1:
        wave_ref[...] = pieces[0][...]
    else:
        me = lax.axis_index("lat")
        span = wave_ref.shape[0] // owners
        for d, distance in enumerate(distances(BACK_ORDER, owners)):
            start = pl.multiple_of((me ^ distance) * span, span)
            wave_ref[pl.ds(start, span), :] = pieces[d][:span, :]
    token = dot(east_ref[...], wave_ref[...]) + kept_ref[...].astype(F32)
    rows, blocks = out.shape[:2]
    for h in range(rows):
        for n in range(blocks):
            p = h * blocks + n
            parts = [token[r * padded : r * padded + units, p * block : (p + 1) * block]
                     for r in range(unit)]
            place = jnp.concatenate(parts, axis=1)
            for c in range(tiles):
                flat_ref[h, n, pl.ds(c, units, stride=tiles), :] = place[:, c * 128 : (c + 1) * 128]
        out[h] = flat_ref[h].reshape(blocks, units * tiles * 128).astype(BF16)


def final_kernel(block, total_ref, first_ref, second_ref):
    owners, per = total_ref.shape[:2]
    blocks = first_ref.shape[1]
    for j in range(owners):
        chunk = total_ref[j].astype(F32)
        out = first_ref if j * per < block else second_ref
        start = j * per % block
        for p in range(2):
            for n in range(blocks):
                at = slice((p * blocks + n) * block, (p * blocks + n + 1) * block)
                out[p, n, start : start + per, :] = chunk[:, at]


VMEM = pl.BlockSpec(memory_space=pltpu.VMEM)


def call(kernel, args, shapes, scratch=(), name=None, in_hbm=0):
    shapes = [shape if isinstance(shape[0], tuple) else (shape, BF16) for shape in shapes]
    kept = [pltpu.with_memory_space_constraint(arg, pltpu.HBM) for arg in args[:in_hbm]]
    return pl.pallas_call(
        kernel,
        out_shape=[jax.ShapeDtypeStruct(shape, kind) for shape, kind in shapes],
        in_specs=[pl.BlockSpec(memory_space=pltpu.HBM)] * in_hbm + [VMEM] * (len(args) - in_hbm),
        out_specs=[VMEM] * len(shapes),
        scratch_shapes=list(scratch),
        name=name,
        compiler_params=pltpu.CompilerParams(vmem_limit_bytes=24 << 20),
    )(*kept, *args[in_hbm:])


def swap(order, pieces, owners):
    return [
        lax.ppermute(piece, "lat", [(i, i ^ d) for i in range(owners)]) if d else piece
        for d, piece in zip(distances(order, owners), pieces)
    ]


def local(tokens, cotangent, first_weight, first_bias, second_weight, relu_mask, shrink_mask):
    batches, rows, blocks, flat_east = tokens.shape
    block = first_weight.shape[2]
    cells = flat_east // block
    owners = lax.axis_size("lat")
    wave_dev = WAVES // owners
    group = group_of(wave_dev)
    groups = wave_dev // group
    north = rows * owners
    width = blocks * block
    field = rows * width
    span = 2 * wave_dev
    factor = 1.0 / math.sqrt(north * WAVES)

    lanes = math.lcm(block, 128)
    unit, tiles = lanes // block, lanes // 128
    units = cells // unit
    padded = -(-units // 16) * 16
    geo = (owners, block, units, padded, tiles, unit)
    east = east_rows(cells, WAVES, owners).reshape(2 * WAVES, units, unit).swapaxes(1, 2)
    east = np.pad(east, ((0, 0), (0, 0), (0, padded - units))).reshape(2 * WAVES, unit * padded)
    east_back = jnp.asarray(east.T, BF16)
    east = jnp.asarray(east, BF16)
    table = north_rows(owners, rows, group)
    forward = jnp.asarray(table, BF16)
    backward = jnp.asarray(table.transpose(0, 2, 1), BF16)

    def by_mode(mask):
        mask = mask.astype(BF16).reshape(2, blocks, groups, group, north, block)
        return mask.transpose(0, 2, 4, 3, 1, 5).reshape(2, wave_dev * north, width)

    def diagonal(weight):
        eye = jnp.eye(blocks, dtype=weight.dtype)
        spread = weight[:, :, :, None, :] * eye[None, :, None, :, None]
        return spread.reshape(2, width, width)

    per = -(-2 * block // owners)
    pairwise = owners in (2, 4, 8) and (2 * group) % 16 == 0 and per * owners == 2 * block

    flat = (rows, blocks, flat_east)
    shapes = [(span, 2 * field)] * owners if pairwise else [(owners * span, 2 * field)]
    *waves, kept = call(
        functools.partial(send_kernel, geo),
        [tokens.reshape(flat), cotangent.reshape(flat), east],
        shapes + [(unit * padded, field)],
        [pltpu.VMEM((2, rows, blocks, units * tiles, 128), F32),
         pltpu.VMEM((unit * padded, 2 * field), BF16),
         pltpu.VMEM((owners * span, 2 * field), BF16), pltpu.VMEM((2,) + flat, BF16),
         pltpu.VMEM(east.shape, BF16), pltpu.SemaphoreType.DMA((3,))], "send", 3,
    )

    if pairwise:
        extra = -(-(per + 1) // 16) * 16 - per
        modes = (2, wave_dev * north, width)
        relu, shrink, weights, bias = call(
            functools.partial(ready_kernel, (groups, group, north, blocks, block)),
            [relu_mask, shrink_mask, first_weight, second_weight, first_bias],
            [modes, modes, (4, width, width), (2, width)], name="ready",
        )
        consts = [forward, backward, weights, bias, relu, shrink]
        pieces = waves
        part = 2 * group
        pieces = call(
            functools.partial(mix_kernel, (owners, groups, rows, blocks, width, per)),
            swap(GO_ORDER, pieces, owners) + consts, [(span + per + extra, field)] * owners,
            [pltpu.VMEM((groups, owners * part, 2 * field), BF16),
             pltpu.VMEM((groups, owners * part, field), BF16),
             pltpu.VMEM((2 * block, field), F32)], "mix",
        )
        pieces = swap(BACK_ORDER, pieces, owners)
        chunk, bias_grad = call(
            functools.partial(sum_kernel, (span, per, block, factor)), pieces,
            [(owners, per, field), ((2, blocks, block), F32)], name="total",
        )
        totals = lax.all_to_all(chunk, "lat", split_axis=0, concat_axis=0, tiled=True)
    else:
        weights = jnp.concatenate([diagonal(first_weight), diagonal(second_weight)])
        bias = first_bias.reshape(2, width)
        consts = [forward, backward, weights, bias, by_mode(relu_mask), by_mode(shrink_mask)]
        waves = waves[0].reshape(owners, span, 2 * field)
        waves = lax.all_to_all(waves, "lat", split_axis=0, concat_axis=0, tiled=True)
        waves = waves.reshape(owners, groups, 2 * group, 2 * field).swapaxes(0, 1)
        sent, grads, biases = [], 0.0, 0.0
        half = group * north
        for g in range(groups):
            at = slice(g * half, (g + 1) * half)
            some = consts[:4] + [mask[:, at] for mask in consts[4:]]
            back, grad, row = call(
                functools.partial(mix_whole_kernel, (rows, blocks, width)),
                [waves[g].reshape(owners * 2 * group, 2 * field)] + some,
                [(owners * 2 * group, field), (2 * block, field), (1, field)], name="mix",
            )
            sent.append(back.reshape(owners, 2 * group, field))
            grads, biases = grads + grad.astype(F32), biases + row.astype(F32)
        grads = jnp.pad(grads, ((0, owners * per - 2 * block), (0, 0)))
        biases = jnp.broadcast_to(biases[None], (owners, 1, field))
        sums = jnp.concatenate([grads.reshape(owners, per, field), biases], axis=1)
        sent = jnp.concatenate(sent + [sums.astype(BF16)], axis=1)
        returned = lax.all_to_all(sent, "lat", split_axis=0, concat_axis=0, tiled=True)
        pieces = [returned[:, :span].reshape(owners * span, field)]
        chunk = jnp.sum(returned[:, span:].astype(F32), axis=0) * factor
        chunk = jnp.broadcast_to(chunk.astype(BF16)[None], (owners,) + chunk.shape)
        totals = lax.all_to_all(chunk, "lat", split_axis=0, concat_axis=0, tiled=True)

    (token,) = call(
        functools.partial(token_kernel, geo), [east_back, kept] + pieces, [flat],
        [pltpu.VMEM((owners * span, field), BF16),
         pltpu.VMEM(flat[:2] + (units * tiles, 128), F32)], "token",
    )
    token = token.reshape(batches, rows, blocks, flat_east)
    if pairwise:
        matrix = ((2, blocks, block, block), F32)
        first, second = call(
            functools.partial(final_kernel, block), [totals], [matrix, matrix], name="final",
        )
        return (token, first, bias_grad, second)
    totals = totals.astype(F32)
    grads = totals[:, :per].reshape(owners * per, field)[: 2 * block]
    grads = grads.reshape(2, block, 2, blocks, block).transpose(0, 2, 3, 1, 4)
    bias_grad = totals[0, per].reshape(2, blocks, block)
    return (token, grads[0], bias_grad, grads[1])


def solution(mesh):
    return jax.shard_map(
        local,
        mesh=mesh,
        in_specs=(
            P(None, "lat", "ch", None),
            P(None, "lat", "ch", None),
            P(None, "ch", None, None),
            P(None, "ch", None),
            P(None, "ch", None, None),
            P(None, None, "ch", "lat", None),
            P(None, None, "ch", "lat", None),
        ),
        out_specs=(
            P(None, "lat", "ch", None),
            P(None, "ch", None, None),
            P(None, "ch", None),
            P(None, "ch", None, None),
        ),
        check_vma=False,
    )
```

```python
import functools
import math

import jax
import jax.numpy as jnp
import numpy as np
from jax import lax
from jax.experimental import pallas as pl
from jax.experimental.pallas import tpu as pltpu
from jax.sharding import PartitionSpec as P

WAVES = 256
GO_ORDER = (0, 4, 6, 5, 7, 2, 3, 1)
BACK_ORDER = (0, 6, 7, 4, 5, 2, 3, 1)
BF16 = jnp.bfloat16
F32 = jnp.float32


def group_of(wave_dev):
    return 8 if wave_dev % 8 == 0 else wave_dev


def east_rows(count, waves, owners):
    wave_dev = waves // owners
    group = group_of(wave_dev)
    phase = np.outer(np.arange(waves), np.arange(count)) % count * (2.0 * math.pi / count)
    table = np.stack([np.cos(phase), -np.sin(phase)]) / math.sqrt(count)
    table = table.reshape(2, owners, wave_dev // group, group, count)
    return table.transpose(1, 2, 0, 3, 4).reshape(2 * waves, count)


def north_rows(owners, rows, group):
    cells = owners * rows
    phase = np.outer(np.arange(cells), np.arange(cells)) % cells * (2.0 * math.pi / cells)
    cosine, sine = np.cos(phase) / math.sqrt(cells), np.sin(phase) / math.sqrt(cells)
    table = np.stack([np.stack([cosine, sine], 1), np.stack([-sine, cosine], 1)])
    table = table.reshape(2, cells, 2, owners, rows)
    full = np.einsum("tqsjr,kl->tqkrjsl", table, np.eye(group))
    return full.reshape(2 * group * cells, rows * owners * 2 * group)


def distances(order, owners):
    return [d for d in order if d < owners]


def dot(left, right, form=((1,), (0,))):
    return lax.dot_general(left, right, (form, ((), ())), preferred_element_type=F32)


ROWS, COLS = ((0,), (0,)), ((1,), (1,))


def mix_core(spec_ref, table_ref, back_ref, weight_ref, bias_ref, relu_ref, shrink_ref,
             lay_ref, result_ref):
    groups = spec_ref.shape[1]
    blocks, block = lay_ref.shape[1], lay_ref.shape[3] // 2
    half = table_ref.shape[0] // 2

    def side(value, n):
        return value[:, n * block : (n + 1) * block]

    for f in range(2):
        for g in range(groups):
            modes = dot(table_ref[...], spec_ref[f, g]).astype(BF16)
            for n in range(blocks):
                lay_ref[f, n, g * half : (g + 1) * half, :] = jnp.concatenate(
                    [side(modes[:half], n), side(modes[half:], n)], axis=1)
    products, biases = ([], []), []
    for n in range(blocks):
        modes, up = lay_ref[0, n], lay_ref[1, n] * shrink_ref[n]
        keep = relu_ref[n].astype(F32)
        one, two = weight_ref[0, n], weight_ref[1, n]
        hidden = (keep * (dot(modes, one) + bias_ref[n : n + 1, :].astype(F32))).astype(BF16)
        inner = (keep * dot(up, two, COLS)).astype(BF16)
        lay_ref[0, n] = dot(inner, one, COLS).astype(BF16)
        products[0].append(dot(modes, inner, ROWS))
        products[1].append(dot(hidden, up, ROWS))
        biases.append(jnp.sum(inner.astype(F32), axis=0, keepdims=True))
    for g in range(groups):
        at = slice(g * half, (g + 1) * half)
        parts = [jnp.concatenate([side(lay_ref[0, n, at, :], s) for n in range(blocks)], axis=1)
                 for s in range(2)]
        result_ref[g] = dot(back_ref[...], jnp.concatenate(parts, axis=0)).astype(BF16)

    def split(product):
        real = side(product[:block], 0) + side(product[block:], 1)
        return real, side(product[:block], 1) - side(product[block:], 0)

    rows = []
    for some in products:
        pairs = [split(product) for product in some]
        rows.append(jnp.concatenate([pair[s] for s in range(2) for pair in pairs], axis=1))
    bias = jnp.concatenate([side(row, s) for s in range(2) for row in biases], axis=1)
    return jnp.concatenate(rows, axis=0), bias


def mix_whole_kernel(*refs):
    spec_ref, result_ref, grad_ref, bias_ref, lay_ref = refs[0], *refs[7:]
    gathered, bias = mix_core(spec_ref, *refs[1:7], lay_ref, result_ref)
    grad_ref[...] = gathered.astype(BF16)
    bias_ref[...] = bias.astype(BF16)


def ready_kernel(geo, relu_in, shrink_in, first_in, second_in, bias_in,
                 relu_out, shrink_out, weight_out, bias_out):
    groups, group, north, blocks, block = geo
    for source, out in ((relu_in, relu_out), (shrink_in, shrink_out)):
        for n in range(blocks):
            planes = [source[0, s, n].astype(F32).astype(BF16) for s in range(2)]
            for q in range(north):
                at = slice(q * block, (q + 1) * block)
                row = jnp.concatenate([plane[:, at] for plane in planes], axis=1)
                for g in range(groups):
                    start = (g * north + q) * group
                    out[n, start : start + group, :] = row[g * group : (g + 1) * group]
    for index, source in enumerate((first_in, second_in)):
        for n in range(blocks):
            real, imag = source[0, n], source[1, n]
            weight_out[index, n, :block, :] = jnp.concatenate([real, imag], axis=1)
            weight_out[index, n, block:, :] = jnp.concatenate([-imag, real], axis=1)
    for n in range(blocks):
        parts = [bias_in[s, n : n + 1, :] for s in range(2)]
        bias_out[n : n + 1, :] = jnp.concatenate(parts, axis=1)


def send_kernel(geo, tokens_ref, cotangent_ref, east_ref, *refs):
    owners, block, units, padded, tiles, unit = geo
    outs, kept_ref = refs[:-7], refs[-7]
    flat_ref, grid_ref, wave_ref, fields_ref, table_ref, sems = refs[-6:]
    rows, blocks = tokens_ref.shape[:2]
    field = rows * blocks * block
    copies = [
        pltpu.make_async_copy(tokens_ref, fields_ref.at[0], sems.at[0]),
        pltpu.make_async_copy(cotangent_ref, fields_ref.at[1], sems.at[1]),
        pltpu.make_async_copy(east_ref, table_ref, sems.at[2]),
    ]
    for copy in copies:
        copy.start()
    for f in range(2):
        copies[f].wait()
        source = fields_ref.at[f]
        places = []
        for h in range(rows):
            flat = source[h].astype(F32)
            flat_ref[f, h] = flat.reshape(blocks, units * tiles, 128)
            for n in range(blocks):
                parts = [flat_ref[f, h, n, pl.ds(c, units, stride=tiles), :].astype(BF16)
                         for c in range(tiles)]
                places.append(jnp.concatenate(parts, axis=1))
        for r in range(unit):
            piece = [place[:, r * block : (r + 1) * block] for place in places]
            at = slice(f * field, (f + 1) * field)
            grid_ref[r * padded : r * padded + units, at] = jnp.concatenate(piece, axis=1)
            if padded > units:
                grid_ref[r * padded + units : (r + 1) * padded, at] = jnp.zeros(
                    (padded - units, field), BF16)
    kept_ref[...] = grid_ref[:, field:]
    copies[2].wait()
    waves = dot(table_ref[...], grid_ref[...]).astype(BF16)
    if len(outs) == 1:
        outs[0][...] = waves
        return
    wave_ref[...] = waves
    me = lax.axis_index("lat")
    span = wave_ref.shape[0] // owners
    for d, distance in enumerate(distances(GO_ORDER, owners)):
        start = pl.multiple_of((me ^ distance) * span, span)
        outs[d][...] = wave_ref[pl.ds(start, span), :]


def mix_kernel(geo, *refs):
    owners, groups, rows, width, per = geo
    pieces, consts, outs = refs[:owners], refs[owners : owners + 6], refs[owners + 6 : -4]
    spec_ref, lay_ref, back_ref, grad_ref = refs[-4:]
    me = lax.axis_index("lat")
    part = pieces[0].shape[0] // groups
    for d, distance in enumerate(distances(GO_ORDER, owners)):
        for f in range(2):
            for r in range(rows):
                lane = (f * rows + r) * width
                value = pieces[d][:, lane : lane + width]
                start = pl.multiple_of((r * owners + (me ^ distance)) * part, part)
                for g in range(groups):
                    spec_ref[f, g, pl.ds(start, part), :] = value[g * part : (g + 1) * part]
    grad_ref[...], bias = mix_core(spec_ref, *consts, lay_ref, back_ref)
    span, lanes = part * groups, outs[0].shape[1]
    tiles = rows * width // lanes
    body = tiles * span
    rest = outs[0].shape[0] - body - tiles * per - tiles
    biases = [bias[:, t * lanes : (t + 1) * lanes] for t in range(tiles)]
    biases.append(jnp.zeros((rest, lanes), F32))
    for d, distance in enumerate(distances(BACK_ORDER, owners)):
        for g in range(groups):
            parts = []
            for r in range(rows):
                start = pl.multiple_of((r * owners + (me ^ distance)) * part, part)
                parts.append(back_ref[g, pl.ds(start, part), :])
            row = jnp.concatenate(parts, axis=1)
            for t in range(tiles):
                start = t * span + g * part
                outs[d][start : start + part, :] = row[:, t * lanes : (t + 1) * lanes]
        start = pl.multiple_of((me ^ distance) * per, per)
        chunk = grad_ref[pl.ds(start, per), :]
        parts = [chunk[:, t * lanes : (t + 1) * lanes] for t in range(tiles)]
        outs[d][body:, :] = jnp.concatenate(parts + biases, axis=0).astype(BF16)


def sum_kernel(geo, *refs):
    body, per, tiles, block, factor = geo
    pieces, out, bias_ref = refs[:-2], refs[-2], refs[-1]
    total = pieces[0][body:, :].astype(F32)
    for piece in pieces[1:]:
        total = total + piece[body:, :].astype(F32)
    total = total * factor
    chunk = total[: tiles * per].astype(BF16)
    for d in range(out.shape[0]):
        out[d] = chunk
    blocks = bias_ref.shape[1]
    lead = [total[tiles * per + t : tiles * per + t + 1, :] for t in range(tiles)]
    lead = jnp.concatenate(lead, axis=1)
    for p in range(2):
        for n in range(blocks):
            at = slice((p * blocks + n) * block, (p * blocks + n + 1) * block)
            bias_ref[p, n : n + 1, :] = lead[:, at]


def token_kernel(geo, east_ref, kept_ref, *refs):
    owners, block, units, padded, tiles, unit = geo
    pieces, out, (wave_ref, flat_ref) = refs[:-3], refs[-3], refs[-2:]
    if len(pieces) == 1:
        wave_ref[...] = pieces[0][...]
    else:
        me = lax.axis_index("lat")
        span = wave_ref.shape[0] // owners
        for d, distance in enumerate(distances(BACK_ORDER, owners)):
            start = pl.multiple_of((me ^ distance) * span, span)
            for t in range(wave_ref.shape[1] // 128):
                at = slice(t * 128, (t + 1) * 128)
                wave_ref[pl.ds(start, span), at] = pieces[d][t * span : (t + 1) * span, :]
    token = dot(east_ref[...], wave_ref[...]) + kept_ref[...].astype(F32)
    rows, blocks = out.shape[:2]
    for h in range(rows):
        for n in range(blocks):
            p = h * blocks + n
            parts = [token[r * padded : r * padded + units, p * block : (p + 1) * block]
                     for r in range(unit)]
            place = jnp.concatenate(parts, axis=1)
            for c in range(tiles):
                flat_ref[h, n, pl.ds(c, units, stride=tiles), :] = place[:, c * 128 : (c + 1) * 128]
        out[h] = flat_ref[h].reshape(blocks, units * tiles * 128).astype(BF16)


def final_kernel(block, total_ref, first_ref, second_ref):
    blocks = first_ref.shape[1]
    tiles = 2 * blocks * block // total_ref.shape[2]
    owners, per = total_ref.shape[0], total_ref.shape[1] // tiles
    for j in range(owners):
        chunk = total_ref[j].astype(F32)
        chunk = jnp.concatenate([chunk[t * per : (t + 1) * per] for t in range(tiles)], axis=1)
        out = first_ref if j * per < block else second_ref
        start = j * per % block
        for p in range(2):
            for n in range(blocks):
                at = slice((p * blocks + n) * block, (p * blocks + n + 1) * block)
                out[p, n, start : start + per, :] = chunk[:, at]


VMEM = pl.BlockSpec(memory_space=pltpu.VMEM)


def call(kernel, args, shapes, scratch=(), name=None, in_hbm=0):
    shapes = [shape if isinstance(shape[0], tuple) else (shape, BF16) for shape in shapes]
    kept = [pltpu.with_memory_space_constraint(arg, pltpu.HBM) for arg in args[:in_hbm]]
    return pl.pallas_call(
        kernel,
        out_shape=[jax.ShapeDtypeStruct(shape, kind) for shape, kind in shapes],
        in_specs=[pl.BlockSpec(memory_space=pltpu.HBM)] * in_hbm + [VMEM] * (len(args) - in_hbm),
        out_specs=[VMEM] * len(shapes),
        scratch_shapes=list(scratch),
        name=name,
        compiler_params=pltpu.CompilerParams(vmem_limit_bytes=24 << 20),
    )(*kept, *args[in_hbm:])


def swap(order, pieces, owners):
    return [
        lax.ppermute(piece, "lat", [(i, i ^ d) for i in range(owners)]) if d else piece
        for d, piece in zip(distances(order, owners), pieces)
    ]


def local(tokens, cotangent, first_weight, first_bias, second_weight, relu_mask, shrink_mask):
    batches, rows, blocks, flat_east = tokens.shape
    block = first_weight.shape[2]
    cells = flat_east // block
    owners = lax.axis_size("lat")
    wave_dev = WAVES // owners
    group = group_of(wave_dev)
    groups = wave_dev // group
    north = rows * owners
    width = blocks * block
    field = rows * width
    span = 2 * wave_dev
    factor = 1.0 / math.sqrt(north * WAVES)

    lanes = math.lcm(block, 128)
    unit, tiles = lanes // block, lanes // 128
    units = cells // unit
    padded = -(-units // 16) * 16
    geo = (owners, block, units, padded, tiles, unit)
    east = east_rows(cells, WAVES, owners).reshape(2 * WAVES, units, unit).swapaxes(1, 2)
    east = np.pad(east, ((0, 0), (0, 0), (0, padded - units))).reshape(2 * WAVES, unit * padded)
    east_back = jnp.asarray(east.T, BF16)
    east = jnp.asarray(east, BF16)
    table = north_rows(owners, rows, group)
    forward = jnp.asarray(table, BF16)
    backward = jnp.asarray(table.T, BF16)

    def by_mode(mask):
        mask = mask.astype(BF16).reshape(2, blocks, groups, group, north, block)
        return mask.transpose(1, 2, 4, 3, 0, 5).reshape(blocks, wave_dev * north, 2 * block)

    def as_real(weight):
        real, imag = weight[0], weight[1]
        top = jnp.concatenate([real, imag], axis=2)
        return jnp.concatenate([top, jnp.concatenate([-imag, real], axis=2)], axis=1)

    per = -(-2 * block // owners)
    pairwise = (
        owners in (2, 4, 8) and group % 8 == 0 and per * owners == 2 * block and field % 128 == 0
    )

    flat = (rows, blocks, flat_east)
    modes = (blocks, wave_dev * north, 2 * block)
    spectra = (groups, rows * owners * 2 * group, width)
    lay = pltpu.VMEM((2,) + modes, BF16)
    shapes = [(span, 2 * field)] * owners if pairwise else [(owners * span, 2 * field)]
    *waves, kept = call(
        functools.partial(send_kernel, geo),
        [tokens.reshape(flat), cotangent.reshape(flat), east],
        shapes + [(unit * padded, field)],
        [pltpu.VMEM((2, rows, blocks, units * tiles, 128), F32),
         pltpu.VMEM((unit * padded, 2 * field), BF16),
         pltpu.VMEM((owners * span, 2 * field), BF16), pltpu.VMEM((2,) + flat, BF16),
         pltpu.VMEM(east.shape, BF16), pltpu.SemaphoreType.DMA((3,))], "send", 3,
    )

    if pairwise:
        ready = call(
            functools.partial(ready_kernel, (groups, group, north, blocks, block)),
            [relu_mask, shrink_mask, first_weight, second_weight, first_bias],
            [modes, modes, (2, blocks, 2 * block, 2 * block), (blocks, 2 * block)], name="ready",
        )
        sides = field // 128
        body = sides * span
        extra = -(-sides * (per + 1) // 16) * 16
        relu, shrink, weights, bias = ready
        pieces = call(
            functools.partial(mix_kernel, (owners, groups, rows, width, per)),
            swap(GO_ORDER, waves, owners) + [forward, backward, weights, bias, relu, shrink],
            [(body + extra, 128)] * owners,
            [pltpu.VMEM((2,) + spectra, BF16), lay, pltpu.VMEM(spectra, BF16),
             pltpu.VMEM((2 * block, field), F32)], "mix",
        )
        pieces = swap(BACK_ORDER, pieces, owners)
        chunk, bias_grad = call(
            functools.partial(sum_kernel, (body, per, sides, block, factor)), pieces,
            [(owners, sides * per, 128), ((2, blocks, block), F32)], name="total",
        )
        totals = lax.all_to_all(chunk, "lat", split_axis=0, concat_axis=0, tiled=True)
    else:
        weights = jnp.stack([as_real(first_weight), as_real(second_weight)])
        bias = first_bias.swapaxes(0, 1).reshape(blocks, 2 * block)
        waves = waves[0].reshape(owners, span, 2 * field)
        waves = lax.all_to_all(waves, "lat", split_axis=0, concat_axis=0, tiled=True)
        waves = waves.reshape(owners, groups, 2 * group, 2, rows, width)
        waves = waves.transpose(3, 1, 4, 0, 2, 5).reshape((2,) + spectra)
        sent, grads, biases = call(
            mix_whole_kernel,
            [waves, forward, backward, weights, bias, by_mode(relu_mask), by_mode(shrink_mask)],
            [spectra, (2 * block, field), (1, field)], [lay], "mix",
        )
        sent = sent.reshape(groups, rows, owners, 2 * group, width).transpose(2, 0, 3, 1, 4)
        sent = sent.reshape(owners, span, field)
        grads = jnp.pad(grads, ((0, owners * per - 2 * block), (0, 0)))
        biases = jnp.broadcast_to(biases[None], (owners, 1, field))
        sent = jnp.concatenate([sent, grads.reshape(owners, per, field), biases], axis=1)
        returned = lax.all_to_all(sent, "lat", split_axis=0, concat_axis=0, tiled=True)
        pieces = [returned[:, :span].reshape(owners * span, field)]
        chunk = jnp.sum(returned[:, span:].astype(F32), axis=0) * factor
        chunk = jnp.broadcast_to(chunk.astype(BF16)[None], (owners,) + chunk.shape)
        totals = lax.all_to_all(chunk, "lat", split_axis=0, concat_axis=0, tiled=True)

    (token,) = call(
        functools.partial(token_kernel, geo), [east_back, kept] + pieces, [flat],
        [pltpu.VMEM((owners * span, field), BF16),
         pltpu.VMEM(flat[:2] + (units * tiles, 128), F32)], "token",
    )
    token = token.reshape(batches, rows, blocks, flat_east)
    if pairwise:
        matrix = ((2, blocks, block, block), F32)
        first, second = call(
            functools.partial(final_kernel, block), [totals], [matrix, matrix], name="final",
        )
        return (token, first, bias_grad, second)
    totals = totals.astype(F32)
    grads = totals[:, :per].reshape(owners * per, field)[: 2 * block]
    grads = grads.reshape(2, block, 2, blocks, block).transpose(0, 2, 3, 1, 4)
    bias_grad = totals[0, per].reshape(2, blocks, block)
    return (token, grads[0], bias_grad, grads[1])


def solution(mesh):
    return jax.shard_map(
        local,
        mesh=mesh,
        in_specs=(
            P(None, "lat", "ch", None),
            P(None, "lat", "ch", None),
            P(None, "ch", None, None),
            P(None, "ch", None),
            P(None, "ch", None, None),
            P(None, None, "ch", "lat", None),
            P(None, None, "ch", "lat", None),
        ),
        out_specs=(
            P(None, "lat", "ch", None),
            P(None, "ch", None, None),
            P(None, "ch", None),
            P(None, "ch", None, None),
        ),
        check_vma=False,
    )
```

```python
import functools
import math

import jax
import jax.numpy as jnp
import numpy as np
from jax import lax
from jax.experimental import pallas as pl
from jax.experimental.pallas import tpu as pltpu
from jax.sharding import PartitionSpec as P


WAVES = 256
PAIRWISE = (2, 4, 8)
GO_ORDER = (0, 7, 5, 6, 3, 4, 2, 1)
BACK_ORDER = (0, 5, 7, 3, 4, 6, 2, 1)
BF16 = jnp.bfloat16
F32 = jnp.float32


def group_of(wave_dev):
    return 8 if wave_dev % 8 == 0 else wave_dev


def east_rows(count, waves, owners):
    wave_dev = waves // owners
    group = group_of(wave_dev)
    phase = np.outer(np.arange(waves), np.arange(count)) % count * (2.0 * math.pi / count)
    table = np.stack([np.cos(phase), -np.sin(phase)]) / math.sqrt(count)
    table = table.reshape(2, owners, wave_dev // group, group, count)
    return table.transpose(1, 2, 0, 3, 4).reshape(2 * waves, count)


def north_rows(owners, rows, group):
    cells = owners * rows
    phase = np.outer(np.arange(cells), np.arange(cells)) % cells * (2.0 * math.pi / cells)
    cosine, sine = np.cos(phase) / math.sqrt(cells), np.sin(phase) / math.sqrt(cells)
    table = np.stack([np.stack([cosine, sine], 1), np.stack([-sine, cosine], 1)])
    table = table.reshape(2, cells, 2, owners, rows)
    full = np.einsum("tqsjr,kl->tqkrjsl", table, np.eye(group))
    return full.reshape(2 * group * cells, rows * owners * 2 * group)


def distances(order, owners):
    return [d for d in order if d < owners]


def first_distance(owners):
    return distances(GO_ORDER, owners)[1]


def dot(left, right, form=((1,), (0,))):
    return lax.dot_general(left, right, (form, ((), ())), preferred_element_type=F32)


ROWS, COLS = ((0,), (0,)), ((1,), (1,))


def mix_core(spec_ref, table_ref, back_ref, weight_ref, bias_ref, relu_ref, shrink_ref,
             lay_ref, result_ref):
    groups = spec_ref.shape[1]
    blocks, block = lay_ref.shape[1], lay_ref.shape[3] // 2
    half = table_ref.shape[0] // 2

    def side(value, n):
        return value[:, n * block : (n + 1) * block]

    for f in range(2):
        for g in range(groups):
            modes = dot(table_ref[...], spec_ref[f, g]).astype(BF16)
            for n in range(blocks):
                lay_ref[f, n, g * half : (g + 1) * half, :] = jnp.concatenate(
                    [side(modes[:half], n), side(modes[half:], n)], axis=1)
    products, biases = ([], []), []
    for n in range(blocks):
        modes, up = lay_ref[0, n], lay_ref[1, n] * shrink_ref[n]
        keep = relu_ref[n].astype(F32)
        one, two = weight_ref[0, n], weight_ref[1, n]
        hidden = (keep * (dot(modes, one) + bias_ref[n : n + 1, :].astype(F32))).astype(BF16)
        inner = (keep * dot(up, two, COLS)).astype(BF16)
        lay_ref[0, n] = dot(inner, one, COLS).astype(BF16)
        products[0].append(dot(modes, inner, ROWS))
        products[1].append(dot(hidden, up, ROWS))
        biases.append(jnp.sum(inner.astype(F32), axis=0, keepdims=True))
    for g in range(groups):
        at = slice(g * half, (g + 1) * half)
        parts = [jnp.concatenate([side(lay_ref[0, n, at, :], s) for n in range(blocks)], axis=1)
                 for s in range(2)]
        result_ref[g] = dot(back_ref[...], jnp.concatenate(parts, axis=0)).astype(BF16)

    def split(product):
        real = side(product[:block], 0) + side(product[block:], 1)
        return real, side(product[:block], 1) - side(product[block:], 0)

    rows = []
    for some in products:
        pairs = [split(product) for product in some]
        rows.append(jnp.concatenate([pair[s] for s in range(2) for pair in pairs], axis=1))
    bias = jnp.concatenate([side(row, s) for s in range(2) for row in biases], axis=1)
    return jnp.concatenate(rows, axis=0), bias


def mix_whole_kernel(*refs):
    spec_ref, result_ref, grad_ref, bias_ref, lay_ref = refs[0], *refs[7:]
    gathered, bias = mix_core(spec_ref, *refs[1:7], lay_ref, result_ref)
    grad_ref[...] = gathered.astype(BF16)
    bias_ref[...] = bias.astype(BF16)


def ready_kernel(geo, relu_in, shrink_in, first_in, second_in, bias_in,
                 relu_out, shrink_out, weight_out, bias_out):
    groups, group, north, blocks, block = geo
    for source, out in ((relu_in, relu_out), (shrink_in, shrink_out)):
        for n in range(blocks):
            planes = [source[0, s, n].astype(F32).astype(BF16) for s in range(2)]
            for q in range(north):
                at = slice(q * block, (q + 1) * block)
                row = jnp.concatenate([plane[:, at] for plane in planes], axis=1)
                for g in range(groups):
                    start = (g * north + q) * group
                    out[n, start : start + group, :] = row[g * group : (g + 1) * group]
    for index, source in enumerate((first_in, second_in)):
        for n in range(blocks):
            real, imag = source[0, n], source[1, n]
            weight_out[index, n, :block, :] = jnp.concatenate([real, imag], axis=1)
            weight_out[index, n, block:, :] = jnp.concatenate([-imag, real], axis=1)
    for n in range(blocks):
        parts = [bias_in[s, n : n + 1, :] for s in range(2)]
        bias_out[n : n + 1, :] = jnp.concatenate(parts, axis=1)


def send_kernel(geo, tokens_ref, cotangent_ref, east_ref, out_ref, grid_ref,
                flat_ref, fields_ref, table_ref, sems):
    owners, block, units, padded, tiles, unit = geo
    rows, blocks = tokens_ref.shape[:2]
    field = rows * blocks * block
    span = out_ref.shape[0]
    copies = []
    for f, source in enumerate((tokens_ref, cotangent_ref)):
        for h in range(rows):
            copies.append((source.at[h], fields_ref.at[f, h]))
    if span < east_ref.shape[0]:
        start = pl.multiple_of((lax.axis_index("lat") ^ first_distance(owners)) * span, span)
        copies.append((east_ref.at[pl.ds(start, span)], table_ref))
    else:
        copies.append((east_ref, table_ref))
    copies = [pltpu.make_async_copy(a, b, sems.at[i]) for i, (a, b) in enumerate(copies)]
    for copy in copies:
        copy.start()
    for f in range(2):
        places = []
        for h in range(rows):
            copies[f * rows + h].wait()
            flat = fields_ref[f, h].astype(F32)
            flat_ref[f, h] = flat.reshape(blocks, units * tiles, 128)
            for n in range(blocks):
                parts = [flat_ref[f, h, n, pl.ds(c, units, stride=tiles), :].astype(BF16)
                         for c in range(tiles)]
                places.append(jnp.concatenate(parts, axis=1))
        for r in range(unit):
            piece = [place[:, r * block : (r + 1) * block] for place in places]
            at = slice(f * field, (f + 1) * field)
            grid_ref[r * padded : r * padded + units, at] = jnp.concatenate(piece, axis=1)
            if padded > units:
                grid_ref[r * padded + units : (r + 1) * padded, at] = jnp.zeros(
                    (padded - units, field), BF16)
    copies[-1].wait()
    out_ref[...] = dot(table_ref[...], grid_ref[...]).astype(BF16)


def rest_kernel(owners, east_ref, grid_ref, *refs):
    outs, table_ref, sems = refs[:-2], refs[-2], refs[-1]
    span = outs[0].shape[0]
    me = lax.axis_index("lat")
    copies = []
    for d, distance in enumerate(d for d in distances(GO_ORDER, owners) if d != first_distance(owners)):
        start = pl.multiple_of((me ^ distance) * span, span)
        copies.append(pltpu.make_async_copy(
            east_ref.at[pl.ds(start, span)], table_ref.at[pl.ds(d * span, span)], sems.at[d]))
    for copy in copies:
        copy.start()
    for copy in copies:
        copy.wait()
    waves = dot(table_ref[...], grid_ref[...]).astype(BF16)
    for d, out in enumerate(outs):
        out[...] = waves[d * span : (d + 1) * span]


def mix_kernel(geo, *refs):
    owners, groups, rows, width, per = geo
    pieces, consts, outs = refs[:owners], refs[owners : owners + 6], refs[owners + 6 : -4]
    spec_ref, lay_ref, back_ref, grad_ref = refs[-4:]
    me = lax.axis_index("lat")
    part = pieces[0].shape[0] // groups
    for d, distance in enumerate(distances(GO_ORDER, owners)):
        for f in range(2):
            for r in range(rows):
                lane = (f * rows + r) * width
                value = pieces[d][:, lane : lane + width]
                start = pl.multiple_of((r * owners + (me ^ distance)) * part, part)
                for g in range(groups):
                    spec_ref[f, g, pl.ds(start, part), :] = value[g * part : (g + 1) * part]
    grad_ref[...], bias = mix_core(spec_ref, *consts, lay_ref, back_ref)
    span, lanes = part * groups, outs[0].shape[1]
    tiles = rows * width // lanes
    body = tiles * span
    rest = outs[0].shape[0] - body - tiles * per - tiles
    biases = [bias[:, t * lanes : (t + 1) * lanes] for t in range(tiles)]
    biases.append(jnp.zeros((rest, lanes), F32))
    for d, distance in enumerate(distances(BACK_ORDER, owners)):
        for g in range(groups):
            parts = []
            for r in range(rows):
                start = pl.multiple_of((r * owners + (me ^ distance)) * part, part)
                parts.append(back_ref[g, pl.ds(start, part), :])
            row = jnp.concatenate(parts, axis=1)
            for t in range(tiles):
                start = t * span + g * part
                outs[d][start : start + part, :] = row[:, t * lanes : (t + 1) * lanes]
        start = pl.multiple_of((me ^ distance) * per, per)
        chunk = grad_ref[pl.ds(start, per), :]
        parts = [chunk[:, t * lanes : (t + 1) * lanes] for t in range(tiles)]
        outs[d][body:, :] = jnp.concatenate(parts + biases, axis=0).astype(BF16)


def sum_kernel(geo, *refs):
    body, per, tiles, block, factor = geo
    pieces, out, bias_ref = refs[:-2], refs[-2], refs[-1]
    total = pieces[0][body:, :].astype(F32)
    for piece in pieces[1:]:
        total = total + piece[body:, :].astype(F32)
    total = total * factor
    chunk = total[: tiles * per].astype(BF16)
    for d in range(out.shape[0]):
        out[d] = chunk
    blocks = bias_ref.shape[1]
    lead = [total[tiles * per + t : tiles * per + t + 1, :] for t in range(tiles)]
    lead = jnp.concatenate(lead, axis=1)
    for p in range(2):
        for n in range(blocks):
            at = slice((p * blocks + n) * block, (p * blocks + n + 1) * block)
            bias_ref[p, n : n + 1, :] = lead[:, at]


def token_kernel(geo, east_ref, grid_ref, *refs):
    owners, block, units, padded, tiles, unit = geo
    pieces, out, (wave_ref, flat_ref) = refs[:-3], refs[-3], refs[-2:]
    if len(pieces) == 1:
        wave_ref[...] = pieces[0][...]
    else:
        me = lax.axis_index("lat")
        span = wave_ref.shape[0] // owners
        for d, distance in enumerate(distances(BACK_ORDER, owners)):
            start = pl.multiple_of((me ^ distance) * span, span)
            for t in range(wave_ref.shape[1] // 128):
                at = slice(t * 128, (t + 1) * 128)
                wave_ref[pl.ds(start, span), at] = pieces[d][t * span : (t + 1) * span, :]
    field = wave_ref.shape[1]
    token = dot(east_ref[...], wave_ref[...]) + grid_ref[:, field:].astype(F32)
    rows, blocks = out.shape[:2]
    for h in range(rows):
        for n in range(blocks):
            p = h * blocks + n
            parts = [token[r * padded : r * padded + units, p * block : (p + 1) * block]
                     for r in range(unit)]
            place = jnp.concatenate(parts, axis=1)
            for c in range(tiles):
                flat_ref[h, n, pl.ds(c, units, stride=tiles), :] = place[:, c * 128 : (c + 1) * 128]
        out[h] = flat_ref[h].reshape(blocks, units * tiles * 128).astype(BF16)


def final_kernel(block, total_ref, first_ref, second_ref):
    blocks = first_ref.shape[1]
    tiles = 2 * blocks * block // total_ref.shape[2]
    owners, per = total_ref.shape[0], total_ref.shape[1] // tiles
    for j in range(owners):
        chunk = total_ref[j].astype(F32)
        chunk = jnp.concatenate([chunk[t * per : (t + 1) * per] for t in range(tiles)], axis=1)
        out = first_ref if j * per < block else second_ref
        start = j * per % block
        for p in range(2):
            for n in range(blocks):
                at = slice((p * blocks + n) * block, (p * blocks + n + 1) * block)
                out[p, n, start : start + per, :] = chunk[:, at]


VMEM = pl.BlockSpec(memory_space=pltpu.VMEM)


def call(kernel, args, shapes, scratch=(), in_hbm=0):
    shapes = [shape if isinstance(shape[0], tuple) else (shape, BF16) for shape in shapes]
    kept = [pltpu.with_memory_space_constraint(arg, pltpu.HBM) for arg in args[:in_hbm]]
    return pl.pallas_call(
        kernel,
        out_shape=[jax.ShapeDtypeStruct(shape, kind) for shape, kind in shapes],
        in_specs=[pl.BlockSpec(memory_space=pltpu.HBM)] * in_hbm + [VMEM] * (len(args) - in_hbm),
        out_specs=[VMEM] * len(shapes),
        scratch_shapes=list(scratch),
        compiler_params=pltpu.CompilerParams(vmem_limit_bytes=24 << 20),
    )(*kept, *args[in_hbm:])


def swap(order, pieces, owners):
    got = []
    for d, piece in zip(distances(order, owners), pieces):
        pairs = [(i, i ^ d) for i in range(owners)]
        got.append(lax.ppermute(piece, "lat", pairs) if d else piece)
    return got


def local(tokens, cotangent, first_weight, first_bias, second_weight, relu_mask, shrink_mask):
    batches, rows, blocks, flat_east = tokens.shape
    block = first_weight.shape[2]
    cells = flat_east // block
    owners = lax.axis_size("lat")
    wave_dev = WAVES // owners
    group = group_of(wave_dev)
    groups = wave_dev // group
    north = rows * owners
    width = blocks * block
    field = rows * width
    span = 2 * wave_dev
    factor = 1.0 / math.sqrt(north * WAVES)

    lanes = math.lcm(block, 128)
    unit, tiles = lanes // block, lanes // 128
    units = cells // unit
    padded = -(-units // 16) * 16
    geo = (owners, block, units, padded, tiles, unit)
    east = east_rows(cells, WAVES, owners).reshape(2 * WAVES, units, unit).swapaxes(1, 2)
    east = np.pad(east, ((0, 0), (0, 0), (0, padded - units))).reshape(2 * WAVES, unit * padded)
    east_back = jnp.asarray(east.T, BF16)
    east = jnp.asarray(east, BF16)
    table = north_rows(owners, rows, group)
    forward = jnp.asarray(table, BF16)
    backward = jnp.asarray(table.T, BF16)

    def by_mode(mask):
        mask = mask.astype(BF16).reshape(2, blocks, groups, group, north, block)
        return mask.transpose(1, 2, 4, 3, 0, 5).reshape(blocks, wave_dev * north, 2 * block)

    def as_real(weight):
        real, imag = weight[0], weight[1]
        top = jnp.concatenate([real, imag], axis=2)
        return jnp.concatenate([top, jnp.concatenate([-imag, real], axis=2)], axis=1)

    per = -(-2 * block // owners)
    pairwise = (
        owners in PAIRWISE and group % 8 == 0 and per * owners == 2 * block and field % 128 == 0
    )

    flat = (rows, blocks, flat_east)
    modes = (blocks, wave_dev * north, 2 * block)
    spectra = (groups, rows * owners * 2 * group, width)
    lay = pltpu.VMEM((2,) + modes, BF16)
    ahead = span if pairwise else owners * span
    waves, grid = call(
        functools.partial(send_kernel, geo),
        [tokens.reshape(flat), cotangent.reshape(flat), east],
        [(ahead, 2 * field), (unit * padded, 2 * field)],
        [pltpu.VMEM((2, rows, blocks, units * tiles, 128), F32), pltpu.VMEM((2,) + flat, BF16),
         pltpu.VMEM((ahead, unit * padded), BF16), pltpu.SemaphoreType.DMA((2 * rows + 1,))],
        3,
    )

    if pairwise:
        own, *rest = call(
            functools.partial(rest_kernel, owners), [east, grid],
            [(span, 2 * field)] * (owners - 1),
            [pltpu.VMEM(((owners - 1) * span, unit * padded), BF16),
             pltpu.SemaphoreType.DMA((owners - 1,))], 1,
        )
        waves = [own, waves] + rest
        ready = call(
            functools.partial(ready_kernel, (groups, group, north, blocks, block)),
            [relu_mask, shrink_mask, first_weight, second_weight, first_bias],
            [modes, modes, (2, blocks, 2 * block, 2 * block), (blocks, 2 * block)],
        )
        sides = field // 128
        body = sides * span
        extra = -(-sides * (per + 1) // 16) * 16
        relu, shrink, weights, bias = ready
        pieces = call(
            functools.partial(mix_kernel, (owners, groups, rows, width, per)),
            swap(GO_ORDER, waves, owners) + [forward, backward, weights, bias, relu, shrink],
            [(body + extra, 128)] * owners,
            [pltpu.VMEM((2,) + spectra, BF16), lay, pltpu.VMEM(spectra, BF16),
             pltpu.VMEM((2 * block, field), F32)],
        )
        pieces = swap(BACK_ORDER, pieces, owners)
        chunk, bias_grad = call(
            functools.partial(sum_kernel, (body, per, sides, block, factor)), pieces,
            [(owners, sides * per, 128), ((2, blocks, block), F32)],
        )
        totals = lax.all_to_all(chunk, "lat", split_axis=0, concat_axis=0, tiled=True)
    else:
        weights = jnp.stack([as_real(first_weight), as_real(second_weight)])
        bias = first_bias.swapaxes(0, 1).reshape(blocks, 2 * block)
        waves = waves.reshape(owners, span, 2 * field)
        waves = lax.all_to_all(waves, "lat", split_axis=0, concat_axis=0, tiled=True)
        waves = waves.reshape(owners, groups, 2 * group, 2, rows, width)
        waves = waves.transpose(3, 1, 4, 0, 2, 5).reshape((2,) + spectra)
        sent, grads, biases = call(
            mix_whole_kernel,
            [waves, forward, backward, weights, bias, by_mode(relu_mask), by_mode(shrink_mask)],
            [spectra, (2 * block, field), (1, field)], [lay],
        )
        sent = sent.reshape(groups, rows, owners, 2 * group, width).transpose(2, 0, 3, 1, 4)
        sent = sent.reshape(owners, span, field)
        grads = jnp.pad(grads, ((0, owners * per - 2 * block), (0, 0)))
        biases = jnp.broadcast_to(biases[None], (owners, 1, field))
        sent = jnp.concatenate([sent, grads.reshape(owners, per, field), biases], axis=1)
        returned = lax.all_to_all(sent, "lat", split_axis=0, concat_axis=0, tiled=True)
        pieces = [returned[:, :span].reshape(owners * span, field)]
        chunk = jnp.sum(returned[:, span:].astype(F32), axis=0) * factor
        chunk = jnp.broadcast_to(chunk.astype(BF16)[None], (owners,) + chunk.shape)
        totals = lax.all_to_all(chunk, "lat", split_axis=0, concat_axis=0, tiled=True)

    (token,) = call(
        functools.partial(token_kernel, geo), [east_back, grid] + pieces, [flat],
        [pltpu.VMEM((owners * span, field), BF16),
         pltpu.VMEM(flat[:2] + (units * tiles, 128), F32)],
    )
    token = token.reshape(batches, rows, blocks, flat_east)
    if pairwise:
        matrix = ((2, blocks, block, block), F32)
        first, second = call(functools.partial(final_kernel, block), [totals], [matrix, matrix])
        return (token, first, bias_grad, second)
    totals = totals.astype(F32)
    grads = totals[:, :per].reshape(owners * per, field)[: 2 * block]
    grads = grads.reshape(2, block, 2, blocks, block).transpose(0, 2, 3, 1, 4)
    bias_grad = totals[0, per].reshape(2, blocks, block)
    return (token, grads[0], bias_grad, grads[1])


def solution(mesh):
    step = mapped(local, mesh)
    return step


def mapped(body, mesh):
    return jax.shard_map(
        body,
        mesh=mesh,
        in_specs=(
            P(None, "lat", "ch", None),
            P(None, "lat", "ch", None),
            P(None, "ch", None, None),
            P(None, "ch", None),
            P(None, "ch", None, None),
            P(None, None, "ch", "lat", None),
            P(None, None, "ch", "lat", None),
        ),
        out_specs=(
            P(None, "lat", "ch", None),
            P(None, "ch", None, None),
            P(None, "ch", None),
            P(None, "ch", None, None),
        ),
        check_vma=False,
    )
```

```python
import functools
import math

import jax
import jax.numpy as jnp
import numpy as np
from jax import lax
from jax.experimental import pallas as pl
from jax.experimental.layout import Layout, with_layout_constraint
from jax.experimental.pallas import tpu as pltpu
from jax.sharding import PartitionSpec as P


WAVES = 256
PAIRWISE = (2, 4, 8)
GO_ORDER = (0, 7, 5, 6, 3, 2, 4, 1)
BACK_ORDER = (0, 5, 7, 3, 4, 6, 2, 1)
BF16 = jnp.bfloat16
F32 = jnp.float32


def group_of(wave_dev):
    return 8 if wave_dev % 8 == 0 else wave_dev


def east_rows(count, waves, owners):
    wave_dev = waves // owners
    group = group_of(wave_dev)
    phase = np.outer(np.arange(waves), np.arange(count)) % count * (2.0 * math.pi / count)
    table = np.stack([np.cos(phase), -np.sin(phase)]) / math.sqrt(count)
    table = table.reshape(2, owners, wave_dev // group, group, count)
    return table.transpose(1, 2, 0, 3, 4).reshape(2 * waves, count)


def north_rows(owners, rows, group):
    cells = owners * rows
    phase = np.outer(np.arange(cells), np.arange(cells)) % cells * (2.0 * math.pi / cells)
    cosine, sine = np.cos(phase) / math.sqrt(cells), np.sin(phase) / math.sqrt(cells)
    table = np.stack([np.stack([cosine, sine], 1), np.stack([-sine, cosine], 1)])
    table = table.reshape(2, cells, 2, owners, rows)
    full = np.einsum("tqsjr,kl->tqkrjsl", table, np.eye(group))
    return full.reshape(2 * group * cells, rows * owners * 2 * group)


def distances(order, owners):
    return [d for d in order if d < owners]


def first_distance(owners):
    return distances(GO_ORDER, owners)[1]


def dot(left, right, form=((1,), (0,))):
    return lax.dot_general(left, right, (form, ((), ())), preferred_element_type=F32)


ROWS, COLS = ((0,), (0,)), ((1,), (1,))


def mix_core(spec_ref, table_ref, back_ref, weight_ref, bias_ref, relu_ref, shrink_ref,
             lay_ref, result_ref):
    groups = spec_ref.shape[1]
    blocks, block = lay_ref.shape[1], lay_ref.shape[3] // 2
    half = table_ref.shape[0] // 2

    def side(value, n):
        return value[:, n * block : (n + 1) * block]

    for f in range(2):
        for g in range(groups):
            modes = dot(table_ref[...], spec_ref[f, g]).astype(BF16)
            for n in range(blocks):
                lay_ref[f, n, g * half : (g + 1) * half, :] = jnp.concatenate(
                    [side(modes[:half], n), side(modes[half:], n)], axis=1)
    products, biases = ([], []), []
    for n in range(blocks):
        modes, up = lay_ref[0, n], lay_ref[1, n] * shrink_ref[n]
        keep = relu_ref[n]
        one, two = weight_ref[0, n], weight_ref[1, n]
        hidden = keep * (dot(modes, one) + bias_ref[n : n + 1, :].astype(F32)).astype(BF16)
        inner = keep * dot(up, two, COLS).astype(BF16)
        lay_ref[0, n] = dot(inner, one, COLS).astype(BF16)
        products[0].append(dot(modes, inner, ROWS))
        products[1].append(dot(hidden, up, ROWS))
        biases.append(jnp.sum(inner.astype(F32), axis=0, keepdims=True))
    for g in range(groups):
        at = slice(g * half, (g + 1) * half)
        parts = [jnp.concatenate([side(lay_ref[0, n, at, :], s) for n in range(blocks)], axis=1)
                 for s in range(2)]
        result_ref[g] = dot(back_ref[...], jnp.concatenate(parts, axis=0)).astype(BF16)

    def split(product):
        real = side(product[:block], 0) + side(product[block:], 1)
        return real, side(product[:block], 1) - side(product[block:], 0)

    rows = []
    for some in products:
        pairs = [split(product) for product in some]
        rows.append(jnp.concatenate([pair[s] for s in range(2) for pair in pairs], axis=1))
    bias = jnp.concatenate([side(row, s) for s in range(2) for row in biases], axis=1)
    return jnp.concatenate(rows, axis=0), bias


def mix_whole_kernel(*refs):
    spec_ref, result_ref, grad_ref, bias_ref, lay_ref = refs[0], *refs[7:]
    gathered, bias = mix_core(spec_ref, *refs[1:7], lay_ref, result_ref)
    grad_ref[...] = gathered.astype(BF16)
    bias_ref[...] = bias.astype(BF16)


def ready_kernel(geo, relu_in, shrink_in, first_in, second_in, bias_in,
                 relu_out, shrink_out, weight_out, bias_out):
    groups, group, north, blocks, block = geo
    for source, out in ((relu_in, relu_out), (shrink_in, shrink_out)):
        for n in range(blocks):
            planes = [source[0, s, n].astype(F32).astype(BF16) for s in range(2)]
            for q in range(north):
                at = slice(q * block, (q + 1) * block)
                row = jnp.concatenate([plane[:, at] for plane in planes], axis=1)
                for g in range(groups):
                    start = (g * north + q) * group
                    out[n, start : start + group, :] = row[g * group : (g + 1) * group]
    for index, source in enumerate((first_in, second_in)):
        for n in range(blocks):
            real, imag = source[0, n], source[1, n]
            weight_out[index, n, :block, :] = jnp.concatenate([real, imag], axis=1)
            weight_out[index, n, block:, :] = jnp.concatenate([-imag, real], axis=1)
    for n in range(blocks):
        parts = [bias_in[s, n : n + 1, :] for s in range(2)]
        bias_out[n : n + 1, :] = jnp.concatenate(parts, axis=1)


def send_kernel(geo, tokens_ref, cotangent_ref, east_ref, out_ref, grid_ref,
                flat_ref, fields_ref, table_ref, sems):
    owners, block, units, padded, tiles, unit = geo
    rows, blocks = tokens_ref.shape[0], tokens_ref.shape[1] // (units * tiles)
    field = rows * blocks * block
    span = out_ref.shape[0]
    copies = []
    for f, source in enumerate((tokens_ref, cotangent_ref)):
        for h in range(rows):
            copies.append((source.at[h], fields_ref.at[f, h]))
    if span < east_ref.shape[0]:
        start = pl.multiple_of((lax.axis_index("lat") ^ first_distance(owners)) * span, span)
        copies.append((east_ref.at[pl.ds(start, span)], table_ref))
    else:
        copies.append((east_ref, table_ref))
    copies = [pltpu.make_async_copy(a, b, sems.at[i]) for i, (a, b) in enumerate(copies)]
    for copy in copies:
        copy.start()
    for f in range(2):
        places = []
        for h in range(rows):
            copies[f * rows + h].wait()
            flat_ref[f, h] = fields_ref[f, h].astype(F32)
            for n in range(blocks):
                parts = [
                    flat_ref[f, h, pl.ds(c * blocks + n, units, stride=tiles * blocks), :]
                    for c in range(tiles)
                ]
                parts = [part.astype(BF16) for part in parts]
                places.append(jnp.concatenate(parts, axis=1))
        for r in range(unit):
            piece = [place[:, r * block : (r + 1) * block] for place in places]
            at = slice(f * field, (f + 1) * field)
            grid_ref[r * padded : r * padded + units, at] = jnp.concatenate(piece, axis=1)
            if padded > units:
                grid_ref[r * padded + units : (r + 1) * padded, at] = jnp.zeros(
                    (padded - units, field), BF16)
    copies[-1].wait()
    out_ref[...] = dot(table_ref[...], grid_ref[...]).astype(BF16)


def rest_kernel(owners, east_ref, grid_ref, *refs):
    outs, table_ref, sems = refs[:-2], refs[-2], refs[-1]
    span = outs[0].shape[0]
    me = lax.axis_index("lat")
    copies = []
    for d, distance in enumerate(d for d in distances(GO_ORDER, owners) if d != first_distance(owners)):
        start = pl.multiple_of((me ^ distance) * span, span)
        copies.append(pltpu.make_async_copy(
            east_ref.at[pl.ds(start, span)], table_ref.at[pl.ds(d * span, span)], sems.at[d]))
    for copy in copies:
        copy.start()
    for copy in copies:
        copy.wait()
    waves = dot(table_ref[...], grid_ref[...]).astype(BF16)
    for d, out in enumerate(outs):
        out[...] = waves[d * span : (d + 1) * span]


def mix_kernel(geo, *refs):
    owners, groups, rows, width, per = geo
    pieces, consts, outs = refs[:owners], refs[owners : owners + 6], refs[owners + 6 : -4]
    spec_ref, lay_ref, back_ref, grad_ref = refs[-4:]
    me = lax.axis_index("lat")
    part = pieces[0].shape[0] // groups
    for d, distance in enumerate(distances(GO_ORDER, owners)):
        for f in range(2):
            for r in range(rows):
                lane = (f * rows + r) * width
                value = pieces[d][:, lane : lane + width]
                start = pl.multiple_of((r * owners + (me ^ distance)) * part, part)
                for g in range(groups):
                    spec_ref[f, g, pl.ds(start, part), :] = value[g * part : (g + 1) * part]
    grad_ref[...], bias = mix_core(spec_ref, *consts, lay_ref, back_ref)
    span, lanes = part * groups, outs[0].shape[1]
    tiles = rows * width // lanes
    body = tiles * span
    rest = outs[0].shape[0] - body - tiles * per - tiles
    biases = [bias[:, t * lanes : (t + 1) * lanes] for t in range(tiles)]
    biases.append(jnp.zeros((rest, lanes), F32))
    for d, distance in enumerate(distances(BACK_ORDER, owners)):
        for g in range(groups):
            parts = []
            for r in range(rows):
                start = pl.multiple_of((r * owners + (me ^ distance)) * part, part)
                parts.append(back_ref[g, pl.ds(start, part), :])
            row = jnp.concatenate(parts, axis=1)
            for t in range(tiles):
                start = t * span + g * part
                outs[d][start : start + part, :] = row[:, t * lanes : (t + 1) * lanes]
        start = pl.multiple_of((me ^ distance) * per, per)
        chunk = grad_ref[pl.ds(start, per), :]
        parts = [chunk[:, t * lanes : (t + 1) * lanes] for t in range(tiles)]
        outs[d][body:, :] = jnp.concatenate(parts + biases, axis=0).astype(BF16)


def sum_kernel(geo, *refs):
    body, per, tiles, block, factor = geo
    pieces, out, bias_ref = refs[:-2], refs[-2], refs[-1]
    total = pieces[0][body:, :].astype(F32)
    for piece in pieces[1:]:
        total = total + piece[body:, :].astype(F32)
    total = total * factor
    chunk = total[: tiles * per].astype(BF16)
    for d in range(out.shape[0]):
        out[d] = chunk
    blocks = bias_ref.shape[1]
    lead = [total[tiles * per + t : tiles * per + t + 1, :] for t in range(tiles)]
    lead = jnp.concatenate(lead, axis=1)
    for p in range(2):
        for n in range(blocks):
            at = slice((p * blocks + n) * block, (p * blocks + n + 1) * block)
            bias_ref[p, n : n + 1, :] = lead[:, at]


def token_kernel(geo, east_ref, grid_ref, *refs):
    owners, block, units, padded, tiles, unit = geo
    pieces, out, (wave_ref, flat_ref) = refs[:-3], refs[-3], refs[-2:]
    if len(pieces) == 1:
        wave_ref[...] = pieces[0][...]
    else:
        me = lax.axis_index("lat")
        span = wave_ref.shape[0] // owners
        for d, distance in enumerate(distances(BACK_ORDER, owners)):
            start = pl.multiple_of((me ^ distance) * span, span)
            for t in range(wave_ref.shape[1] // 128):
                at = slice(t * 128, (t + 1) * 128)
                wave_ref[pl.ds(start, span), at] = pieces[d][t * span : (t + 1) * span, :]
    field = wave_ref.shape[1]
    token = dot(east_ref[...], wave_ref[...]) + grid_ref[:, field:].astype(F32)
    rows, blocks = out.shape[:2]
    for h in range(rows):
        for n in range(blocks):
            p = h * blocks + n
            parts = [token[r * padded : r * padded + units, p * block : (p + 1) * block]
                     for r in range(unit)]
            place = jnp.concatenate(parts, axis=1)
            for c in range(tiles):
                flat_ref[h, n, pl.ds(c, units, stride=tiles), :] = place[:, c * 128 : (c + 1) * 128]
        out[h] = flat_ref[h].reshape(blocks, units * tiles * 128).astype(BF16)


def final_kernel(block, total_ref, first_ref, second_ref):
    blocks = first_ref.shape[1]
    tiles = 2 * blocks * block // total_ref.shape[2]
    owners, per = total_ref.shape[0], total_ref.shape[1] // tiles
    for j in range(owners):
        chunk = total_ref[j].astype(F32)
        chunk = jnp.concatenate([chunk[t * per : (t + 1) * per] for t in range(tiles)], axis=1)
        out = first_ref if j * per < block else second_ref
        start = j * per % block
        for p in range(2):
            for n in range(blocks):
                at = slice((p * blocks + n) * block, (p * blocks + n + 1) * block)
                out[p, n, start : start + per, :] = chunk[:, at]


VMEM = pl.BlockSpec(memory_space=pltpu.VMEM)


def call(kernel, args, shapes, scratch=(), in_hbm=0):
    shapes = [shape if isinstance(shape[0], tuple) else (shape, BF16) for shape in shapes]
    kept = [pltpu.with_memory_space_constraint(arg, pltpu.HBM) for arg in args[:in_hbm]]
    return pl.pallas_call(
        kernel,
        out_shape=[jax.ShapeDtypeStruct(shape, kind) for shape, kind in shapes],
        in_specs=[pl.BlockSpec(memory_space=pltpu.HBM)] * in_hbm + [VMEM] * (len(args) - in_hbm),
        out_specs=[VMEM] * len(shapes),
        scratch_shapes=list(scratch),
        compiler_params=pltpu.CompilerParams(vmem_limit_bytes=24 << 20),
    )(*kept, *args[in_hbm:])


def swap(order, pieces, owners):
    got = []
    for d, piece in zip(distances(order, owners), pieces):
        pairs = [(i, i ^ d) for i in range(owners)]
        got.append(lax.ppermute(piece, "lat", pairs) if d else piece)
    return got


def local(tokens, cotangent, first_weight, first_bias, second_weight, relu_mask, shrink_mask):
    batches, rows, blocks, flat_east = tokens.shape
    block = first_weight.shape[2]
    cells = flat_east // block
    owners = lax.axis_size("lat")
    wave_dev = WAVES // owners
    group = group_of(wave_dev)
    groups = wave_dev // group
    north = rows * owners
    width = blocks * block
    field = rows * width
    span = 2 * wave_dev
    factor = 1.0 / math.sqrt(north * WAVES)

    lanes = math.lcm(block, 128)
    unit, tiles = lanes // block, lanes // 128
    units = cells // unit
    padded = -(-units // 16) * 16
    geo = (owners, block, units, padded, tiles, unit)
    east = east_rows(cells, WAVES, owners).reshape(2 * WAVES, units, unit).swapaxes(1, 2)
    east = np.pad(east, ((0, 0), (0, 0), (0, padded - units))).reshape(2 * WAVES, unit * padded)
    east_back = jnp.asarray(east.T, BF16)
    east = jnp.asarray(east, BF16)
    table = north_rows(owners, rows, group)
    forward = jnp.asarray(table, BF16)
    backward = jnp.asarray(table.T, BF16)

    def by_tile(value):
        value = value.reshape(rows, blocks, units * tiles, 128)
        value = with_layout_constraint(value, Layout(major_to_minor=(0, 2, 1, 3)))
        return value.transpose(0, 2, 1, 3).reshape(rows, blocks * units * tiles, 128)

    def by_mode(mask):
        mask = mask.astype(BF16).reshape(2, blocks, groups, group, north, block)
        return mask.transpose(1, 2, 4, 3, 0, 5).reshape(blocks, wave_dev * north, 2 * block)

    def as_real(weight):
        real, imag = weight[0], weight[1]
        top = jnp.concatenate([real, imag], axis=2)
        return jnp.concatenate([top, jnp.concatenate([-imag, real], axis=2)], axis=1)

    per = -(-2 * block // owners)
    pairwise = (
        owners in PAIRWISE and group % 8 == 0 and per * owners == 2 * block and field % 128 == 0
    )

    flat = (rows, blocks, flat_east)
    modes = (blocks, wave_dev * north, 2 * block)
    spectra = (groups, rows * owners * 2 * group, width)
    lay = pltpu.VMEM((2,) + modes, BF16)
    ahead = span if pairwise else owners * span
    waves, grid = call(
        functools.partial(send_kernel, geo),
        [by_tile(tokens), by_tile(cotangent), east],
        [(ahead, 2 * field), (unit * padded, 2 * field)],
        [pltpu.VMEM((2, rows, blocks * units * tiles, 128), F32),
         pltpu.VMEM((2, rows, blocks * units * tiles, 128), BF16),
         pltpu.VMEM((ahead, unit * padded), BF16), pltpu.SemaphoreType.DMA((2 * rows + 1,))],
        3,
    )

    if pairwise:
        own, *rest = call(
            functools.partial(rest_kernel, owners), [east, grid],
            [(span, 2 * field)] * (owners - 1),
            [pltpu.VMEM(((owners - 1) * span, unit * padded), BF16),
             pltpu.SemaphoreType.DMA((owners - 1,))], 1,
        )
        waves = [own, waves] + rest
        ready = call(
            functools.partial(ready_kernel, (groups, group, north, blocks, block)),
            [relu_mask, shrink_mask, first_weight, second_weight, first_bias],
            [modes, modes, (2, blocks, 2 * block, 2 * block), (blocks, 2 * block)],
        )
        sides = field // 128
        body = sides * span
        extra = -(-sides * (per + 1) // 16) * 16
        relu, shrink, weights, bias = ready
        pieces = call(
            functools.partial(mix_kernel, (owners, groups, rows, width, per)),
            swap(GO_ORDER, waves, owners) + [forward, backward, weights, bias, relu, shrink],
            [(body + extra, 128)] * owners,
            [pltpu.VMEM((2,) + spectra, BF16), lay, pltpu.VMEM(spectra, BF16),
             pltpu.VMEM((2 * block, field), F32)],
        )
        pieces = swap(BACK_ORDER, pieces, owners)
        chunk, bias_grad = call(
            functools.partial(sum_kernel, (body, per, sides, block, factor)), pieces,
            [(owners, sides * per, 128), ((2, blocks, block), F32)],
        )
        totals = lax.all_to_all(chunk, "lat", split_axis=0, concat_axis=0, tiled=True)
    else:
        weights = jnp.stack([as_real(first_weight), as_real(second_weight)])
        bias = first_bias.swapaxes(0, 1).reshape(blocks, 2 * block)
        waves = waves.reshape(owners, span, 2 * field)
        waves = lax.all_to_all(waves, "lat", split_axis=0, concat_axis=0, tiled=True)
        waves = waves.reshape(owners, groups, 2 * group, 2, rows, width)
        waves = waves.transpose(3, 1, 4, 0, 2, 5).reshape((2,) + spectra)
        sent, grads, biases = call(
            mix_whole_kernel,
            [waves, forward, backward, weights, bias, by_mode(relu_mask), by_mode(shrink_mask)],
            [spectra, (2 * block, field), (1, field)], [lay],
        )
        sent = sent.reshape(groups, rows, owners, 2 * group, width).transpose(2, 0, 3, 1, 4)
        sent = sent.reshape(owners, span, field)
        grads = jnp.pad(grads, ((0, owners * per - 2 * block), (0, 0)))
        biases = jnp.broadcast_to(biases[None], (owners, 1, field))
        sent = jnp.concatenate([sent, grads.reshape(owners, per, field), biases], axis=1)
        returned = lax.all_to_all(sent, "lat", split_axis=0, concat_axis=0, tiled=True)
        pieces = [returned[:, :span].reshape(owners * span, field)]
        chunk = jnp.sum(returned[:, span:].astype(F32), axis=0) * factor
        chunk = jnp.broadcast_to(chunk.astype(BF16)[None], (owners,) + chunk.shape)
        totals = lax.all_to_all(chunk, "lat", split_axis=0, concat_axis=0, tiled=True)

    (token,) = call(
        functools.partial(token_kernel, geo), [east_back, grid] + pieces, [flat],
        [pltpu.VMEM((owners * span, field), BF16),
         pltpu.VMEM(flat[:2] + (units * tiles, 128), F32)],
    )
    token = token.reshape(batches, rows, blocks, flat_east)
    if pairwise:
        matrix = ((2, blocks, block, block), F32)
        first, second = call(functools.partial(final_kernel, block), [totals], [matrix, matrix])
        return (token, first, bias_grad, second)
    totals = totals.astype(F32)
    grads = totals[:, :per].reshape(owners * per, field)[: 2 * block]
    grads = grads.reshape(2, block, 2, blocks, block).transpose(0, 2, 3, 1, 4)
    bias_grad = totals[0, per].reshape(2, blocks, block)
    return (token, grads[0], bias_grad, grads[1])


def solution(mesh):
    step = mapped(local, mesh)
    return step


def mapped(body, mesh):
    return jax.shard_map(
        body,
        mesh=mesh,
        in_specs=(
            P(None, "lat", "ch", None),
            P(None, "lat", "ch", None),
            P(None, "ch", None, None),
            P(None, "ch", None),
            P(None, "ch", None, None),
            P(None, None, "ch", "lat", None),
            P(None, None, "ch", "lat", None),
        ),
        out_specs=(
            P(None, "lat", "ch", None),
            P(None, "ch", None, None),
            P(None, "ch", None),
            P(None, "ch", None, None),
        ),
        check_vma=False,
    )
```
